32 devices in a mesh: groups: 2 (over y), cand: 4 (over z), tensor: 4 (over x, core).
Axes of the slice: x: 2, y: 2, z: 4, core: 2. Of those that a mesh axis runs over, the one named last changes fastest.
Arguments:
- response_latest_embeddings: bfloat16 [16, 384, 8192], P(('groups', 'cand'), None, 'tensor'), parts along dimension 0, may hold values from -6 to 6
- critic_probe_projector: bfloat16 [8192, 4096], P('cand', 'tensor'), may hold values from -0.0625 to 0.0625
- critic_pair_projector: bfloat16 [8192, 2048], P('cand', 'tensor'), may hold values from -0.0625 to 0.0625
- critic_stored_pairs: bfloat16 [16, 2048, 2048], P(('groups', 'cand'), None, 'tensor'), parts along dimension 0, may hold values from -1000 to 1000
- critic_grading_vector: float32 [4096], P('tensor'), may hold values from -6 to 6
- actor_stored_pairs: bfloat16 [16, 2048, 8, 256], P(('groups', 'cand'), None, 'tensor'), parts along dimension 0, may hold values from -1000 to 1000
- filled_extents: int32 [16], P('groups'), parts along dimension 0, may hold values from 1 to 2048, as said below
- kept_responses: int32 [8], P('groups'), parts along dimension 0, may hold values from 0 to 7, as said below
- actor_latest_probes: bfloat16 [8, 4, 4096], P(('groups', 'cand'), None, 'tensor'), parts along dimension 0, may hold values from -6 to 6
- actor_latest_pairs: bfloat16 [8, 4, 2048], P(('groups', 'cand'), None, 'tensor'), parts along dimension 0, may hold values from -6 to 6
Outputs:
- token_rewards: float32 [16, 384], P(('groups', 'cand')), parts along dimension 0
- actor_mixing_result: bfloat16 [8, 4, 4096], P(('groups', 'cand'), None, 'tensor'), parts along dimension 0
The draws below stay inside these ranges and needn't reach their ends.
There are 2 independent parts, one for each index of `groups`. The reference program is written for one: setup_inputs(seed, part) draws one part's arguments, and reference() takes and returns one part's arrays. A program takes and returns all parts, laid end to end along the dimension named above; an argument that names none is the same for every part. Nothing has to cross between parts.
Inputs may be any that keep to these rules, and one draw needn't show every extreme that they name: `kept_responses`: distinct candidate ids, always including 0 and 7. `filled_extents`: some candidate has exactly 2048 live tokens.
All inputs are finite; a program needn't handle non-finite values.
Results may differ from the reference program's by a relative error of at most 0.012.
The reference program's roundings to bfloat16 on the way count: a program that leaves them out, or rounds other values in their place, can miss the bound.
Values may be sent and summed in bfloat16 or wider, within the bound.
A program may use at most 128 MiB of HBM per device.

```python
import jax
import jax.numpy as jnp
from jax import lax

D = 8192
RQH = 32
RKV = 8
HD = 128
PQH = 32
PKV = 8
CTX = 2048
SPAN = 384
PMAX = 2048
NEW = 4
CANDS = 8
KEEP = 4


def cache_entries(key, cands, length, heads):
    base = jnp.clip(jax.random.normal(key, (cands, length, heads, 2 * HD), jnp.float32), -6.0, 6.0)
    return base


def draw_critic_stored_pairs(key, part):
    values = cache_entries(jax.random.fold_in(key, 21), CANDS, CTX, RKV)
    return values.reshape(CANDS, CTX, RKV * 2 * HD).astype(jnp.bfloat16)


def draw_actor_stored_pairs(key, part):
    return cache_entries(jax.random.fold_in(key, 23), CANDS, PMAX, PKV).astype(jnp.bfloat16)


def draw_filled_extents(key, part):
    key_one, key_two = jax.random.split(jax.random.fold_in(key, 11))
    values = jax.random.randint(key_one, (CANDS,), 1, PMAX + 1)
    full_at = jax.random.randint(key_two, (), 0, CANDS)
    return values.at[full_at].set(PMAX).astype(jnp.int32)


def draw_kept_responses(key, part):
    key_one, key_two = jax.random.split(jax.random.fold_in(key, 13))
    middle = jax.random.permutation(key_one, jnp.arange(1, CANDS - 1, dtype=jnp.int32))[:KEEP - 2]
    chosen_lanes = jnp.concatenate([jnp.array([0, CANDS - 1], jnp.int32), middle])
    return jax.random.permutation(key_two, chosen_lanes).astype(jnp.int32)


def steps_of(rng, extent, cuts, smallest, top_value):
    def one(dim, parts):
        steps = jax.random.uniform(jax.random.fold_in(jax.random.fold_in(rng, 6), dim), (parts,), jnp.float32, smallest / len(cuts), top_value / len(cuts))
        return jnp.repeat(jnp.exp(steps), extent[dim] // parts).reshape((-1,) + (1,) * (len(extent) - dim - 1))

    loudness = one(*cuts[0])
    for cut in cuts[1:]:
        loudness = loudness * one(*cut)
    return loudness


def scatter_about(stream_key, dims, spread, most, cuts=(), kind=jnp.bfloat16):
    values = jax.random.normal(stream_key, dims, jnp.float32) * spread
    if len(cuts) > 0:
        values = steps_of(stream_key, dims, cuts, -0.22, 0.18) * values
    return jnp.clip(values, min=-most, max=most).astype(kind)


def setup_inputs(seed: int = 0, part: int = 0) -> dict:
    splits = jax.random.split(jax.random.key(seed), 11)
    part_keys = jax.random.split(jax.random.fold_in(splits[10], part), 11)
    return {
        "response_latest_embeddings": scatter_about(part_keys[0], (CANDS, SPAN, D), 1.0, 6.0, ((0, 4), (2, 4))),
        "critic_probe_projector": scatter_about(splits[1], (D, RQH * HD), D ** -0.5, 0.0625, ((0, 4), (1, 4))),
        "critic_pair_projector": scatter_about(splits[2], (D, RKV * 2 * HD), D ** -0.5, 0.0625, ((0, 4), (1, 4))),
        "critic_stored_pairs": draw_critic_stored_pairs(jax.random.fold_in(jax.random.fold_in(splits[10], part), 71), part),
        "critic_grading_vector": scatter_about(splits[4], (RQH * HD,), 1.0, 6.0, ((0, 4),), jnp.float32),
        "actor_stored_pairs": draw_actor_stored_pairs(jax.random.fold_in(jax.random.fold_in(splits[10], part), 71), part),
        "filled_extents": draw_filled_extents(jax.random.fold_in(jax.random.fold_in(splits[10], part), 71), part),
        "kept_responses": draw_kept_responses(jax.random.fold_in(jax.random.fold_in(splits[10], part), 71), part),
        "actor_latest_probes": scatter_about(part_keys[8], (KEEP, NEW, PQH * HD), 1.0, 6.0, ((0, 4), (2, 4))),
        "actor_latest_pairs": scatter_about(part_keys[9], (KEEP, NEW, PKV * 2 * HD), 1.0, 6.0, ((0, 4), (2, 4))),
    }


masked_value = -1e30


def reference(response_latest_embeddings, critic_probe_projector, critic_pair_projector, critic_stored_pairs, critic_grading_vector, actor_stored_pairs, filled_extents, kept_responses, actor_latest_probes, actor_latest_pairs):
    tok_rows = response_latest_embeddings.reshape(CANDS * SPAN, D)
    query_heads = jnp.dot(tok_rows, critic_probe_projector, preferred_element_type=jnp.float32).astype(jnp.bfloat16)
    keyval = jnp.dot(tok_rows, critic_pair_projector, preferred_element_type=jnp.float32).astype(jnp.bfloat16)
    query_heads = query_heads.reshape(CANDS, SPAN, RKV, RQH // RKV, HD)
    keyval = keyval.reshape(CANDS, SPAN, RKV, 2 * HD)
    cached = critic_stored_pairs.reshape(CANDS, CTX, RKV, 2 * HD)
    causal = jnp.arange(SPAN)[:, None] >= jnp.arange(SPAN)[None, :]
    visible = jnp.concatenate([jnp.ones((SPAN, CTX), dtype=bool), causal], axis=1)

    def score_one(entry_pair):
        queries, fresh_keys, old_keys = entry_pair
        every_key = jnp.concatenate([old_keys, fresh_keys], axis=0).astype(jnp.float32)
        scores = jnp.einsum("tkgd,skd->kgts", queries.astype(jnp.float32), every_key[..., :HD]) * HD ** -0.5
        scores = jnp.where(visible, scores, masked_value)
        rounded = lax.optimization_barrier(jax.nn.softmax(scores, axis=-1).astype(jnp.bfloat16))
        heads_out = jnp.einsum("kgts,skd->tkgd", rounded.astype(jnp.float32), every_key[..., HD:])
        return jnp.dot(heads_out.reshape(SPAN, RQH * HD), critic_grading_vector, precision=lax.Precision.HIGHEST)

    token_rewards = lax.map(score_one, (query_heads, keyval, cached))

    causal_new = jnp.arange(NEW)[:, None] >= jnp.arange(NEW)[None, :]

    def generate_for_lane(entry_pair):
        chosen_lanes, queries, fresh_keys = entry_pair
        old_keys = lax.dynamic_index_in_dim(actor_stored_pairs, chosen_lanes, 0, keepdims=False)
        live_len = lax.dynamic_index_in_dim(filled_extents, chosen_lanes, 0, keepdims=False)
        living_response_flags = jnp.arange(PMAX) < live_len
        visible_new = jnp.concatenate([jnp.broadcast_to(living_response_flags, (NEW, PMAX)), causal_new], axis=1)
        every_key = jnp.concatenate([old_keys, fresh_keys.reshape(NEW, PKV, 2 * HD)], axis=0).astype(jnp.float32)
        heads_in = queries.reshape(NEW, PKV, PQH // PKV, HD).astype(jnp.float32)
        scores = jnp.einsum("ikgd,skd->kgis", heads_in, every_key[..., :HD]) * HD ** -0.5
        scores = jnp.where(visible_new, scores, masked_value)
        weights = jax.nn.softmax(scores, axis=-1)
        heads_out = jnp.einsum("kgis,skd->ikgd", weights, every_key[..., HD:])
        return heads_out.reshape(NEW, PQH * HD).astype(jnp.bfloat16)

    actor_mixing_result = lax.map(generate_for_lane, (kept_responses, actor_latest_probes, actor_latest_pairs))
    return token_rewards, actor_mixing_result
```

```python
import functools

import jax
import jax.numpy as jnp
from jax import lax
from jax.experimental import pallas as pl
from jax.experimental.pallas import tpu as pltpu
from jax.sharding import PartitionSpec as P

HD = 128
CW = 2 * HD
SPLIT = 2
AHEAD = 4
LAG = 4
TILES = 4
MESH = pl.DeviceIdType.MESH

masked_value = -1e30
LOG2E = 1.4426950408889634


def when(cond, body):
    pl.when(cond)(body)


def reward_kernel(
    nz, nt, per_group,
    x_ref, wq_ref, wkv_ref, cache_ref, pcache_ref,
    grade_ref, probes_ref, pairs_ref, kept_ref, extents_ref,
    reward_ref, mix_ref,
    xbuf, sbuf, wbuf, cbuf, pbuf, acts, sres, part, toks,
    qall, pall, qsel, psel, qrow, krow, vrow, placed, given, mine,
    load_sem, right_sem, left_sem, line_sem, pair_send, pair_recv,
    x_right, x_left, x_line, x_psend, x_precv,
    s_send, s_recv, sx_right, sx_left, sx_line, sx_psend, sx_precv,
    r_send, r_recv, t_send, t_recv,
    q_send, q_recv, p_send, p_recv, give_send, give_recv,
):
    nchunk, depth, _ = wbuf.shape
    nv = nchunk * SPLIT
    dz = depth // nz
    sub = dz // SPLIT
    nx = nt // 2
    cands, span, _ = part.shape
    rows = cands * span
    dx = depth // nt
    qchunks = per_group * HD // CW
    groups = nchunk // (1 + qchunks)
    qrows = rows // TILES
    per_cand = TILES // cands
    srows = rows // nv
    vx = max(2, nv // 4 * 2)
    sx = vx - 1
    sp_step = []
    for i in range(TILES):
        at = nv if i == TILES - 1 else max(nv - TILES + 1 + i, 4 * groups + 1)
        sp_step.append(at if at < nv else nv)
    off_step = [s + 1 if s + 1 < nv else nv + 1 for s in sp_step]

    def whole16(n):
        return max(sub // 2, int(round(n / 16)) * 16)

    share_first = whole16(sub * 2 / 3)
    share_mid = whole16(sub * 7 / 12)
    share_last = sub // 2

    y = lax.axis_index("groups")
    z = lax.axis_index("cand")
    t = lax.axis_index("tensor")
    x = t // 2
    c = t - 2 * x
    at_end = (z == 0) | (z == nz - 1)
    beside = (z == 1) | (z == nz - 2)
    inner = jnp.where(z == 0, 1, nz - 2)
    outer = jnp.where(z == 1, 0, nz - 1)

    def is_away(p):
        return (p < 2 * groups) & (lax.rem(p, 2) == 1)

    def is_query(p):
        return (p >= 2 * groups) | (lax.rem(p, 2) == 1)

    def columns(p):
        if p < 2 * groups:
            g, j = p // 2, (p % 2) * qchunks
        else:
            g, j = divmod(p - 2 * groups, qchunks - 1)
            j += 1
        if j == 0:
            return wkv_ref.at[:, pl.ds(g * CW, CW)]
        return wq_ref.at[:, pl.ds((g * qchunks + j - 1) * CW, CW)]

    own_rows = pl.ds(pl.multiple_of(z * dz, dz), dz)
    loads = [
        pltpu.make_async_copy(columns(p), wbuf.at[p, own_rows, :], load_sem.at[p])
        for p in range(nchunk)
    ]
    x_load = pltpu.make_async_copy(x_ref, xbuf.at[t], load_sem.at[nchunk])
    c_load = pltpu.make_async_copy(cache_ref, cbuf, load_sem.at[nchunk + 1])
    p_loads = [
        pltpu.make_async_copy(pcache_ref.at[b], pbuf, load_sem.at[nchunk + 2 + b])
        for b in range(cands)
    ]
    loads[0].start()
    x_load.start()
    for p in range(1, nchunk):
        loads[p].start()
    p_loads[0].start()
    c_load.start()

    barrier = pltpu.get_barrier_semaphore()

    def greet(device):
        pl.semaphore_signal(barrier, inc=1, device_id=device, device_id_type=MESH)

    greet({"groups": 1 - y})

    def greet_cand(d, carry):
        greet({"cand": lax.rem(z + d, nz)})
        return carry

    def greet_tensor(d, carry):
        greet({"tensor": lax.rem(t + d, nt)})
        return carry

    lax.fori_loop(1, nz, greet_cand, 0)
    lax.fori_loop(1, nt, greet_tensor, 0)
    pl.semaphore_wait(barrier, nz + nt - 1)

    def remote(src, dst, send, recv, device):
        return pltpu.make_async_remote_copy(
            src_ref=src, dst_ref=dst, send_sem=send, recv_sem=recv,
            device_id=device, device_id_type=MESH,
        )

    def hop(src, dst, body):
        first = (src == 0) | (src == nz - 1)
        last = (dst == 0) | (dst == nz - 1)
        when(first, lambda: body(share_first))
        when(last, lambda: body(share_last))
        when(jnp.logical_not(first | last), lambda: body(share_mid))

    def piece(v, o, start, size):
        p = v // SPLIT
        base = o * dz + (v - p * SPLIT) * sub + start
        return wbuf.at[p, pl.ds(pl.multiple_of(base, 16), size), :]

    def go_right(v, o, s):
        ref = piece(v, o, y * (sub - s), s)
        return remote(ref, ref, right_sem.at[v, o], line_sem.at[v, o], {"cand": z + 1})

    def go_left(v, o, s):
        ref = piece(v, o, y * (sub - s), s)
        return remote(ref, ref, left_sem.at[v, o], line_sem.at[v, o], {"cand": z - 1})

    def to_pair(v, o, s):
        ref = piece(v, o, y * s, sub - s)
        return remote(ref, ref, pair_send.at[v, o], pair_recv.at[v, o], {"groups": 1 - y})

    def from_pair(v, o, s):
        ref = piece(v, o, (1 - y) * s, sub - s)
        return remote(ref, ref, pair_send.at[v, o], pair_recv.at[v, o], {"groups": 1 - y})

    def sends_right(p):
        return (z < nz - 1) & jnp.logical_not(is_away(p) & (z + 1 == nz - 1))

    def sends_left(p):
        return (z > 0) & jnp.logical_not(is_away(p) & (z - 1 == 0))

    def send_own(v):
        p = v // SPLIT
        when(sends_right(p), lambda: hop(z, z + 1, lambda s: go_right(v, z, s).start()))
        when(sends_left(p), lambda: hop(z, z - 1, lambda s: go_left(v, z, s).start()))

    def relay(v, first, last):
        p = v // SPLIT
        here = jnp.logical_not(is_away(p) & at_end)

        def one(d, carry):
            @pl.when((z - d >= 0) & here)
            def _():
                o = z - d
                hop(z - 1, z, lambda s: go_right(v, o, s).wait_recv())
                when(sends_right(p), lambda: hop(z, z + 1, lambda s: go_right(v, o, s).start()))
                hop(z - 1, z, lambda s: to_pair(v, o, s).start())

            @pl.when((z + d < nz) & here)
            def _():
                o = z + d
                hop(z + 1, z, lambda s: go_left(v, o, s).wait_recv())
                when(sends_left(p), lambda: hop(z, z - 1, lambda s: go_left(v, o, s).start()))
                hop(z + 1, z, lambda s: to_pair(v, o, s).start())

            return carry

        lax.fori_loop(first, last, one, 0)

    def drain(v):
        p = v // SPLIT

        def one(o, carry):
            when(
                (o <= z) & sends_right(p),
                lambda: hop(z, z + 1, lambda s: go_right(v, o, s).wait_send()),
            )
            when(
                (o >= z) & sends_left(p),
                lambda: hop(z, z - 1, lambda s: go_left(v, o, s).wait_send()),
            )

            @pl.when((o != z) & jnp.logical_not(is_away(p) & at_end))
            def _():
                hop(jnp.where(o < z, z - 1, z + 1), z, lambda s: to_pair(v, o, s).wait_send())

            return carry

        lax.fori_loop(0, nz, one, 0)

    def row_gather(buf, at, right, left, line, psend, precv):
        def block(o, core):
            return buf.at[2 * o + core, at, :]

        def to_right(o):
            return remote(block(o, c), block(o, c), right(o), line(o), {"tensor": t + 2})

        def to_left(o):
            return remote(block(o, c), block(o, c), left(o), line(o), {"tensor": t - 2})

        def across(o, core):
            return remote(
                block(o, core), block(o, core), psend(o), precv(o), {"tensor": 2 * x + 1 - c}
            )

        def begin():
            when(x < nx - 1, lambda: to_right(x).start())
            when(x > 0, lambda: to_left(x).start())
            across(x, c).start()

        def finish():
            for d in range(1, nx):
                @pl.when(x - d >= 0)
                def _(d=d):
                    to_right(x - d).wait_recv()
                    when(x < nx - 1, lambda: to_right(x - d).start())
                    across(x - d, c).start()

                @pl.when(x + d < nx)
                def _(d=d):
                    to_left(x + d).wait_recv()
                    when(x > 0, lambda: to_left(x + d).start())
                    across(x + d, c).start()

            for o in range(nx):
                across(o, 1 - c).wait_recv()

        def settle():
            for o in range(nx):
                across(o, c).wait_send()
                when((o <= x) & (x < nx - 1), lambda o=o: to_right(o).wait_send())
                when((o >= x) & (x > 0), lambda o=o: to_left(o).wait_send())

        return begin, finish, settle

    x_begin, x_finish, x_settle = row_gather(
        xbuf, pl.ds(0, rows), lambda o: x_right.at[o], lambda o: x_left.at[o],
        lambda o: x_line.at[o], lambda o: x_psend.at[o], lambda o: x_precv.at[o],
    )

    def span_rows(j):
        return pl.ds(pl.multiple_of(j * srows, srows), srows)

    def lend(j):
        at = span_rows(j)
        return remote(
            xbuf.at[t, at, :], sbuf.at[t, at, :], s_send.at[j], s_recv.at[j], {"cand": inner}
        )

    def borrowed(j):
        return row_gather(
            sbuf, span_rows(j), lambda o: sx_right.at[j, o], lambda o: sx_left.at[j, o],
            lambda o: sx_line.at[j, o], lambda o: sx_psend.at[j, o], lambda o: sx_precv.at[j, o],
        )

    def tile_rows(i):
        return pl.ds(pl.multiple_of(i * qrows, qrows), qrows)

    def give_back(g, i):
        at = tile_rows(i)
        return remote(
            sres.at[g, at, :], acts.at[2 * g + 1, at, :], r_send.at[g, i], r_recv.at[g, i],
            {"cand": outer},
        )

    def get_back(g, i):
        at = acts.at[2 * g + 1, tile_rows(i), :]
        return remote(at, at, r_send.at[g, i], r_recv.at[g, i], {"cand": inner})

    def each(first, last, body):
        def one(j, carry):
            body(j)
            return carry

        lax.fori_loop(first, last, one, 0)

    def others(body):
        each(1, nz, lambda d: body(lax.rem(z + d, nz)))

    def ask(src, buf, send, recv, o, lands):
        return remote(src, buf.at[lands], send.at[o], recv.at[lands], {"cand": o})

    def ask_all(o):
        ask(probes_ref, qall, q_send, q_recv, o, z).start()
        ask(pairs_ref, pall, p_send, p_recv, o, z).start()

    others(ask_all)
    for v in range(AHEAD):
        if v % SPLIT == 0:
            loads[v // SPLIT].wait()
        send_own(v)
        if v == 0:
            x_load.wait()
            x_begin()
        when(at_end, lambda v=v: lend(v).start())
    for p in range(-(-AHEAD // SPLIT), nchunk):
        loads[p].wait()
    part[...] = jnp.zeros_like(part)

    lanes, fresh, _ = probes_ref.shape
    kv_here = pcache_ref.shape[2]
    tokens = pcache_ref.shape[1]
    pgroup = probes_ref.shape[2] // HD // kv_here
    prow = pgroup * fresh

    def match(o, l, b):
        same = kept_ref[o * lanes + l] == z * cands + b
        return jnp.where(same, 1.0, 0.0)

    def pick(o, q, kv, fresh_start):
        for b in range(cands):
            for l in range(lanes):
                m = match(o, l, b)
                if fresh_start and l == 0:
                    qsel[b] = q(l) * m
                    psel[b] = kv(l) * m
                else:
                    qsel[b] += q(l) * m
                    psel[b] += kv(l) * m

    def policy():
        pick(
            z, lambda l: probes_ref[l].astype(jnp.float32),
            lambda l: pairs_ref[l].astype(jnp.float32), True,
        )

        def take(o):
            ask(probes_ref, qall, q_send, q_recv, o, o).wait_recv()
            ask(pairs_ref, pall, p_send, p_recv, o, o).wait_recv()
            pick(
                o, lambda l: qall[o, l].astype(jnp.float32),
                lambda l: pall[o, l].astype(jnp.float32), False,
            )
            ask(probes_ref, qall, q_send, q_recv, o, z).wait_send()
            ask(pairs_ref, pall, p_send, p_recv, o, z).wait_send()

        others(take)
        for b in range(cands):
            for g in range(kv_here):
                for h in range(pgroup):
                    head = (g * pgroup + h) * HD
                    qrow[g * prow + h * fresh:g * prow + (h + 1) * fresh, :] = (
                        qsel[b, :, head:head + HD]
                    )
                krow[g * fresh:(g + 1) * fresh, :] = psel[b, :, g * CW:g * CW + HD]
                vrow[g * fresh:(g + 1) * fresh, :] = psel[b, :, g * CW + HD:(g + 1) * CW]
            p_loads[b].wait()
            old_k = pbuf[:, :, :HD].reshape(tokens * kv_here, HD)
            old_v = pbuf[:, :, HD:].reshape(tokens * kv_here, HD)
            q = qrow[...].astype(jnp.bfloat16)
            dims = (((1,), (1,)), ((), ()))
            s1 = lax.dot_general(q, old_k, dims, preferred_element_type=jnp.float32)
            s2 = lax.dot_general(
                q, krow[...].astype(jnp.bfloat16), dims, preferred_element_type=jnp.float32
            )
            r1 = lax.broadcasted_iota(jnp.int32, s1.shape, 0)
            c1 = lax.broadcasted_iota(jnp.int32, s1.shape, 1)
            r2 = lax.broadcasted_iota(jnp.int32, s2.shape, 0)
            c2 = lax.broadcasted_iota(jnp.int32, s2.shape, 1)
            live = extents_ref[z * cands + b]
            seen1 = (c1 % kv_here == r1 // prow) & (c1 < live * kv_here)
            seen2 = (c2 // fresh == r2 // prow) & (c2 % fresh <= r2 % fresh)
            s1 = jnp.where(seen1, s1, masked_value)
            s2 = jnp.where(seen2, s2, masked_value)
            top = jnp.maximum(
                jnp.max(s1, axis=1, keepdims=True), jnp.max(s2, axis=1, keepdims=True)
            )
            e1 = jnp.exp((s1 - top) * HD ** -0.5)
            e2 = jnp.exp((s2 - top) * HD ** -0.5)
            total = jnp.sum(e1, axis=1, keepdims=True) + jnp.sum(e2, axis=1, keepdims=True)
            out = jnp.dot(e1.astype(jnp.bfloat16), old_v, preferred_element_type=jnp.float32)
            out = out + jnp.dot(
                e2.astype(jnp.bfloat16), vrow[...].astype(jnp.bfloat16),
                preferred_element_type=jnp.float32,
            )
            if b + 1 < cands:
                p_loads[b + 1].start()
            out = out / total
            for o in range(nz):
                for l in range(lanes):
                    given_to = (out * match(o, l, b)).astype(jnp.bfloat16)
                    if b == 0:
                        placed[o, l] = given_to
                    else:
                        placed[o, l] += given_to

    def give(o):
        return remote(
            placed.at[o], given.at[z], give_send.at[o], give_recv.at[z], {"cand": o}
        )

    def get(o):
        return remote(
            placed.at[o], given.at[o], give_send.at[o], give_recv.at[o], {"cand": o}
        )

    def collect():
        mine[...] = placed[z].astype(jnp.float32)

        def add(o):
            get(o).wait_recv()
            mine[...] += given[o].astype(jnp.float32)
            give(o).wait_send()

        others(add)
        for l in range(lanes):
            for g in range(kv_here):
                for h in range(pgroup):
                    head = (g * pgroup + h) * HD
                    start = g * prow + h * fresh
                    mix_ref[l, :, head:head + HD] = (
                        mine[l, start:start + fresh, :].astype(mix_ref.dtype)
                    )

    policy()

    def multiply(buf, p, at):
        acc = jnp.dot(buf[0, at, :], wbuf[p, :dx, :], preferred_element_type=jnp.float32)
        for s in range(1, nt):
            acc = acc + jnp.dot(
                buf[s, at, :], wbuf[p, s * dx:(s + 1) * dx, :],
                preferred_element_type=jnp.float32,
            )
        return acc.astype(jnp.bfloat16)

    def project(p):
        @pl.when(jnp.logical_not(is_away(p) & at_end))
        def _():
            def take(d):
                o = jnp.where(d < z, d, d + 1)
                src = jnp.where(o < z, z - 1, z + 1)
                for r in range(SPLIT):
                    hop(src, z, lambda s: from_pair(p * SPLIT + r, o, s).wait_recv())

            each(0, nz - 1, take)
            row_tile = rows // 3

            def tile(r):
                at = pl.ds(pl.multiple_of(r * row_tile, row_tile), row_tile)
                acts[p, at, :] = multiply(xbuf, p, at)

            each(0, rows // row_tile, tile)

    def project_lent(i):
        def arrive(j):
            borrowed(j)[1]()

        each((i * nv + TILES - 1) // TILES, ((i + 1) * nv + TILES - 1) // TILES, arrive)
        at = tile_rows(i)

        def one(g):
            sres[g, at, :] = multiply(sbuf, 2 * g + 1, at)

        each(0, groups, one)

    def attend(p, i):
        away = p < 2 * groups
        late = p - 2 * groups
        g = jnp.where(away, p // 2, late // max(qchunks - 1, 1))
        j = jnp.where(away, qchunks - 1, lax.rem(late, max(qchunks - 1, 1)))
        head0 = (g * qchunks + j) * 2
        base = pl.multiple_of(g * CW, CW)
        b = i // per_cand
        start = (i - b * per_cand) * qrows
        at = tile_rows(i)
        new_at = pl.ds(pl.multiple_of(b * span, span), span)
        old_k = cbuf[b, :, pl.ds(base, HD)]
        old_v = cbuf[b, :, pl.ds(pl.multiple_of(base + HD, HD), HD)]
        new_k = acts[2 * g, new_at, :HD]
        new_v = acts[2 * g, new_at, HD:]
        q = jnp.concatenate([acts[p, at, :HD], acts[p, at, HD:]], axis=0)
        dims = (((1,), (1,)), ((), ()))
        s1 = lax.dot_general(q, old_k, dims, preferred_element_type=jnp.float32)
        s2 = lax.dot_general(q, new_k, dims, preferred_element_type=jnp.float32)
        ri = lax.broadcasted_iota(jnp.int32, s2.shape, 0)
        ci = lax.broadcasted_iota(jnp.int32, s2.shape, 1)
        ri = jnp.where(ri >= qrows, ri - qrows, ri) + start
        s2 = jnp.where(ri >= ci, s2, masked_value)
        top = jnp.maximum(jnp.max(s1, axis=1, keepdims=True), jnp.max(s2, axis=1, keepdims=True))
        scale = HD ** -0.5 * LOG2E
        e1 = jnp.exp2((s1 - top) * scale)
        e2 = jnp.exp2((s2 - top) * scale)
        total = jnp.sum(e1, axis=1, keepdims=True) + jnp.sum(e2, axis=1, keepdims=True)
        o = jnp.dot(e1.astype(jnp.bfloat16), old_v, preferred_element_type=jnp.float32)
        o = o + jnp.dot(e2.astype(jnp.bfloat16), new_v, preferred_element_type=jnp.float32)
        o = o / total
        part[b, pl.ds(pl.multiple_of(start, qrows), qrows), :] += (
            o[:qrows] * grade_ref[pl.ds(head0, 1), :]
            + o[qrows:] * grade_ref[pl.ds(head0 + 1, 1), :]
        )

    def count(steps, test):
        total = jnp.int32(0)
        for s in steps:
            total = total + test(s).astype(jnp.int32)
        return total

    def step(v, carry):
        ongoing = v < nv

        @pl.when(v + AHEAD < nv)
        def _():
            send_own(v + AHEAD)
            when(at_end, lambda: lend(v + AHEAD).start())

        when(ongoing, lambda: relay(v, 1, 2))

        @pl.when(v == 1)
        def _():
            others(lambda o: give(o).start())

        when(v == 3, collect)

        @pl.when(beside & ongoing & (v >= sx))
        def _():
            def start(j):
                lend(j).wait_recv()
                borrowed(j)[0]()

            each(jnp.where(v == sx, 0, v), v + 1, start)

        @pl.when(v == vx)
        def _():
            x_finish()
            c_load.wait()

        even = lax.rem(v, 2) == 0
        half = v // 2

        @pl.when(even & (v >= vx))
        def _():
            each(jnp.where(v == vx, 0, half - 1), half, project)

        when(ongoing, lambda: relay(v, 2, min(3, nz)))

        @pl.when(beside)
        def _():
            lo = count(sp_step, lambda s: s < v)
            hi = count(sp_step, lambda s: s <= v)
            each(lo, hi, project_lent)

        whole = jnp.logical_not(even) & (v >= vx + 1)
        first = jnp.where(v == vx + 1, 0, half - 1) * TILES
        ours = jnp.where(whole, half * TILES - first, 0)
        lo = count(off_step, lambda s: s < v)
        hi = count(off_step, lambda s: s <= v)
        theirs = jnp.where(at_end, (hi - lo) * groups, 0)

        def unit(n):
            mine_first = n < ours
            k = n - ours
            i_away = lo + k // groups
            g_away = k - (k // groups) * groups
            p = jnp.where(mine_first, (first + n) // TILES, 2 * g_away + 1)
            i = jnp.where(mine_first, lax.rem(first + n, TILES), i_away)
            when(jnp.logical_not(mine_first), lambda: get_back(g_away, i_away).wait_recv())

            @pl.when(jnp.logical_not(mine_first) | (is_query(p) & jnp.logical_not(is_away(p) & at_end)))
            def _():
                attend(p, i)

        each(0, ours + theirs, unit)

        when(ongoing, lambda: relay(v, 3, nz))

        @pl.when(beside)
        def _():
            lo = count(sp_step, lambda s: s < v)
            hi = count(sp_step, lambda s: s <= v)
            each(lo, hi, lambda i: each(0, groups, lambda g: give_back(g, i).start()))

        when(v >= LAG, lambda: drain(v - LAG))
        return carry

    lax.fori_loop(0, nv + 2, step, 0)

    for b in range(cands):
        toks[t, b:b + 1, :] = jnp.sum(part[b].T, axis=0, keepdims=True)
    each(nv + 2 - LAG, nv, drain)
    x_settle()

    def tell(o):
        return remote(toks.at[t], toks.at[t], t_send.at[o], t_recv.at[t], {"tensor": o})

    def hear(o):
        return remote(toks.at[o], toks.at[o], t_send.at[o], t_recv.at[o], {"tensor": o})

    each(1, nt, lambda d: tell(lax.rem(t + d, nt)).start())
    when(at_end, lambda: each(0, nv, lambda j: lend(j).wait_send()))

    @pl.when(beside)
    def _():
        each(0, nv, lambda j: borrowed(j)[2]())
        each(0, groups, lambda g: each(0, TILES, lambda i: give_back(g, i).wait_send()))

    def heard(d):
        o = lax.rem(t + d, nt)
        hear(o).wait_recv()
        tell(o).wait_send()

    each(1, nt, heard)
    total = toks[0]
    for o in range(1, nt):
        total = total + toks[o]
    reward_ref[...] = total


def local(
    nz, nt,
    response_latest_embeddings,
    critic_probe_projector,
    critic_pair_projector,
    critic_stored_pairs,
    critic_grading_vector,
    actor_stored_pairs,
    filled_extents,
    kept_responses,
    actor_latest_probes,
    actor_latest_pairs,
):
    cands, span, dx = response_latest_embeddings.shape
    rows = cands * span
    wq, wkv = critic_probe_projector, critic_pair_projector
    depth = wq.shape[0] * nz
    groups = wkv.shape[1] // CW
    per_group = wq.shape[1] // HD // groups
    nchunk = (wq.shape[1] + wkv.shape[1]) // CW
    nv = nchunk * SPLIT
    nx = nt // 2
    lanes, fresh, pwidth = actor_latest_probes.shape
    kv_here = actor_stored_pairs.shape[2]
    prows = pwidth // HD * fresh
    bf16, f32 = jnp.bfloat16, jnp.float32
    vmem = pl.BlockSpec(memory_space=pltpu.VMEM)
    smem = pl.BlockSpec(memory_space=pltpu.SMEM)
    anywhere = pl.BlockSpec(memory_space=pl.ANY)
    dma = pltpu.SemaphoreType.DMA
    token_rewards, mixed = pl.pallas_call(
        functools.partial(reward_kernel, nz, nt, per_group),
        out_shape=(
            jax.ShapeDtypeStruct((cands, span), f32),
            jax.ShapeDtypeStruct(actor_latest_probes.shape, bf16),
        ),
        in_specs=[anywhere] * 5 + [vmem] * 3 + [smem] * 2,
        out_specs=(vmem, vmem),
        scratch_shapes=[
            pltpu.VMEM((nt, rows, dx), bf16),
            pltpu.VMEM((nt, rows, dx), bf16),
            pltpu.VMEM((nchunk, depth, CW), bf16),
            pltpu.VMEM(critic_stored_pairs.shape, bf16),
            pltpu.VMEM(actor_stored_pairs.shape[1:], bf16),
            pltpu.VMEM((nchunk, rows, CW), bf16),
            pltpu.VMEM((groups, rows, CW), bf16),
            pltpu.VMEM((cands, span, HD), f32),
            pltpu.VMEM((nt, cands, span), f32),
            pltpu.VMEM((nz,) + actor_latest_probes.shape, bf16),
            pltpu.VMEM((nz,) + actor_latest_pairs.shape, bf16),
            pltpu.VMEM((cands, fresh, pwidth), f32),
            pltpu.VMEM((cands, fresh, actor_latest_pairs.shape[2]), f32),
            pltpu.VMEM((prows, HD), f32),
            pltpu.VMEM((kv_here * fresh, HD), f32),
            pltpu.VMEM((kv_here * fresh, HD), f32),
            pltpu.VMEM((nz, lanes, prows, HD), bf16),
            pltpu.VMEM((nz, lanes, prows, HD), bf16),
            pltpu.VMEM((lanes, prows, HD), f32),
            dma((nchunk + 2 + cands,)),
            dma((nv, nz)), dma((nv, nz)), dma((nv, nz)), dma((nv, nz)), dma((nv, nz)),
            dma((nx,)), dma((nx,)), dma((nx,)), dma((nx,)), dma((nx,)),
            dma((nv,)), dma((nv,)),
            dma((nv, nx)), dma((nv, nx)), dma((nv, nx)), dma((nv, nx)), dma((nv, nx)),
            dma((groups, TILES)), dma((groups, TILES)),
            dma((nt,)), dma((nt,)),
            dma((nz,)), dma((nz,)), dma((nz,)), dma((nz,)), dma((nz,)), dma((nz,)),
        ],
        compiler_params=pltpu.CompilerParams(
            collective_id=0, has_side_effects=True, vmem_limit_bytes=67043328
        ),
    )(
        response_latest_embeddings.reshape(rows, dx), wq, wkv, critic_stored_pairs,
        actor_stored_pairs, critic_grading_vector.reshape(-1, HD), actor_latest_probes,
        actor_latest_pairs, kept_responses, filled_extents,
    )
    return token_rewards, mixed


def solution(mesh):
    placed = (
        P(("groups", "cand"), None, "tensor"),
        P("cand", "tensor"),
        P("cand", "tensor"),
        P(("groups", "cand"), None, "tensor"),
        P("tensor"),
        P(("groups", "cand"), None, "tensor", None),
        P("groups"),
        P("groups"),
        P(("groups", "cand"), None, "tensor"),
        P(("groups", "cand"), None, "tensor"),
    )
    return jax.shard_map(
        functools.partial(local, mesh.shape["cand"], mesh.shape["tensor"]),
        mesh=mesh,
        in_specs=placed,
        out_specs=(P(("groups", "cand"), None), P(("groups", "cand"), None, "tensor")),
        check_vma=False,
    )
```

```python
import functools

import jax
import jax.numpy as jnp
from jax import lax
from jax.experimental import pallas as pl
from jax.experimental.pallas import tpu as pltpu
from jax.sharding import PartitionSpec as P

HD = 128
CW = 2 * HD
SPLIT = 2
AHEAD = 2
LEAD = 1
BEHIND = 2
LAG = 2 * SPLIT
TILES = 4
BLOCKS = 3
ROOM = 4.0
KEYS = 512
MIDDLE = 0.594
COST = {"multiply": 1.3, "attend": 1.7, "lent": 1.0}
MESH = pl.DeviceIdType.MESH

masked_value = -1e30
LOG2E = 1.4426950408889634


def when(cond, body):
    pl.when(cond)(body)


def lookup(table, n):
    value = jnp.int32(table[0])
    for k in range(1, len(table)):
        if table[k] != table[k - 1]:
            value = jnp.where(n >= k, table[k], value)
    return value


def plan(nchunk, stride, cands):
    nv = nchunk * SPLIT
    groups = nchunk // stride
    early = stride - 1
    last = nchunk - 1
    first_away = groups * early
    x_step = [max(1, k * nv // 12) for k in (2, 4, 6)]
    lent_step = [k * nv // 12 for k in (6, 8, 11)] + [nv]
    per_cand = TILES // cands
    todo_p = sorted(
        (max(2 * SPLIT * (p + 1) + 2, 2 * x_step[r]), p, r)
        for p in range(nchunk) for r in range(BLOCKS)
    )
    todo_p = [(min(w, 2 * nv + (p == last and r > 0)), p, r) for w, p, r in todo_p]
    todo_s = sorted(
        (max(min(2 * SPLIT * (first_away + g + 1) + 2, 2 * nv), 2 * lent_step[i]), i, g)
        for g in range(groups) for i in range(TILES)
    )
    todo_a = [
        (p, i) for p in range(nchunk) for i in range(TILES) if p >= first_away or p % early
    ]
    units = {"multiply": [], "attend": [], "lent": []}
    ends = {k: [0] for k in units}
    done = {}
    lent_at = {}

    def blocks(first, last):
        return range(first * BLOCKS // TILES, -(-last * BLOCKS // TILES))

    for w in range(2 * (nv + 2)):
        left = ROOM if w < 2 * nv - 1 else 1e9
        while todo_p and todo_p[0][0] <= w and left > 0:
            _, p, r = todo_p.pop(0)
            units["multiply"].append((p, r))
            done[p, r] = w
            left -= COST["multiply"]
        while todo_s and todo_s[0][0] <= w and left > 0:
            _, i, g = todo_s[0]
            if (first_away + g, 0) not in done:
                break
            todo_s.pop(0)
            units["lent"].append((g, i))
            lent_at[g, i] = w // 2
            left -= COST["lent"]
        if w in (2 * nv - 1, 2 * nv):
            left = 2 * COST["attend"] - 0.1 if w < 2 * nv else 0
        while todo_a and left > 0:
            ready = None
            for p, i in todo_a:
                b = i // per_cand
                need = [(p, r) for r in blocks(i, i + 1)]
                kv = p // early * early if p < first_away else (p - first_away) * early
                need += [(kv, r) for r in blocks(b * per_cand, (b + 1) * per_cand)]
                if all(n in done for n in need):
                    ready = (p, i)
                    break
            if ready is None:
                break
            todo_a.remove(ready)
            units["attend"].append(ready)
            left -= COST["attend"]
        for k in units:
            ends[k].append(len(units[k]))
    assert not (todo_p or todo_s or todo_a)
    back = sorted(
        (lent_at[u] + 2 if lent_at[u] + 2 <= nv else nv + 1, u[1], u[0]) for u in units["lent"]
    )
    units["back"] = [(g, i) for _, i, g in back]
    ends["back"] = [sum(b[0] < v for b in back) for v in range(nv + 3)]
    return units, ends, x_step


def reward_kernel(
    nz, nt, per_group,
    x_ref, wq_ref, wkv_ref, cache_ref, pcache_ref,
    grade_ref, probes_ref, pairs_ref, kept_ref, extents_ref,
    reward_ref, mix_ref,
    xbuf, sbuf, wbuf, cbuf, pbuf, acts, sres, part, toks,
    qall, pall, qsel, psel, qrow, krow, vrow, placed, given, mine,
    load_sem, right_sem, left_sem, line_sem, pair_send, pair_recv,
    x_right, x_left, x_line, x_psend, x_precv,
    s_send, s_recv, sx_right, sx_left, sx_line, sx_psend, sx_precv,
    r_send, r_recv, t_send, t_recv,
    q_send, q_recv, p_send, p_recv, give_send, give_recv,
):
    nchunk, depth, _ = wbuf.shape
    nv = nchunk * SPLIT
    dz = depth // nz
    sub = dz // SPLIT
    nx = nt // 2
    cands, span, _ = part.shape
    rows = cands * span
    dx = depth // nt
    qchunks = per_group * HD // CW
    groups = nchunk // (1 + qchunks)
    qrows = rows // TILES
    per_cand = TILES // cands
    lots = 2 * nchunk
    per_lot = SPLIT // 2
    srows = rows // lots
    stride = 1 + qchunks
    row_block = rows // BLOCKS
    first_away = groups * qchunks
    units, ends, x_step = plan(nchunk, stride, cands)

    def whole16(n):
        return max(sub // 2, int(round(n / 16)) * 16)

    share_first = whole16(sub * 2 / 3)
    share_mid = whole16(sub * MIDDLE)
    share_last = sub // 2

    y = lax.axis_index("groups")
    z = lax.axis_index("cand")
    t = lax.axis_index("tensor")
    x = t // 2
    c = t - 2 * x
    at_end = (z == 0) | (z == nz - 1)
    beside = (z == 1) | (z == nz - 2)
    inner = jnp.where(z == 0, 1, nz - 2)
    outer = jnp.where(z == 1, 0, nz - 1)

    def is_away(p):
        return p >= first_away

    def group_of(p):
        return jnp.where(is_away(p), p - first_away, p // qchunks)

    def columns(p):
        if p >= first_away:
            g, j = p - first_away, qchunks - 1
        else:
            g, j = p // qchunks, p % qchunks - 1
        if j < 0:
            return wkv_ref.at[:, pl.ds(g * CW, CW)]
        return wq_ref.at[:, pl.ds((g * qchunks + j) * CW, CW)]

    own_rows = pl.ds(pl.multiple_of(z * dz, dz), dz)
    loads = [
        pltpu.make_async_copy(columns(p), wbuf.at[p, own_rows, :], load_sem.at[p])
        for p in range(nchunk)
    ]
    x_load = pltpu.make_async_copy(x_ref, xbuf.at[t], load_sem.at[nchunk])
    c_load = pltpu.make_async_copy(cache_ref, cbuf, load_sem.at[nchunk + 1])
    p_loads = [
        pltpu.make_async_copy(pcache_ref.at[b], pbuf, load_sem.at[nchunk + 2 + b])
        for b in range(cands)
    ]
    loads[0].start()
    x_load.start()
    for p in range(1, nchunk):
        loads[p].start()
    p_loads[0].start()
    c_load.start()

    barrier = pltpu.get_barrier_semaphore()

    def greet(device):
        pl.semaphore_signal(barrier, inc=1, device_id=device, device_id_type=MESH)

    greet({"groups": 1 - y})

    def greet_cand(d, carry):
        greet({"cand": lax.rem(z + d, nz)})
        return carry

    def greet_tensor(d, carry):
        greet({"tensor": lax.rem(t + d, nt)})
        return carry

    lax.fori_loop(1, nz, greet_cand, 0)
    lax.fori_loop(1, nt, greet_tensor, 0)
    pl.semaphore_wait(barrier, nz + nt - 1)

    def remote(src, dst, send, recv, device):
        return pltpu.make_async_remote_copy(
            src_ref=src, dst_ref=dst, send_sem=send, recv_sem=recv,
            device_id=device, device_id_type=MESH,
        )

    def hop(src, dst, body):
        first = (src == 0) | (src == nz - 1)
        last = (dst == 0) | (dst == nz - 1)
        when(first, lambda: body(share_first))
        when(last, lambda: body(share_last))
        when(jnp.logical_not(first | last), lambda: body(share_mid))

    def piece(v, o, start, size):
        p = v // SPLIT
        base = o * dz + (v - p * SPLIT) * sub + start
        return wbuf.at[p, pl.ds(pl.multiple_of(base, 16), size), :]

    def go_right(v, o, s):
        ref = piece(v, o, y * (sub - s), s)
        return remote(ref, ref, right_sem.at[v, o], line_sem.at[v, o], {"cand": z + 1})

    def go_left(v, o, s):
        ref = piece(v, o, y * (sub - s), s)
        return remote(ref, ref, left_sem.at[v, o], line_sem.at[v, o], {"cand": z - 1})

    def to_pair(v, o, s):
        ref = piece(v, o, y * s, sub - s)
        return remote(ref, ref, pair_send.at[v, o], pair_recv.at[v, o], {"groups": 1 - y})

    def from_pair(v, o, s):
        ref = piece(v, o, (1 - y) * s, sub - s)
        return remote(ref, ref, pair_send.at[v, o], pair_recv.at[v, o], {"groups": 1 - y})

    def sends_right(p):
        return (z < nz - 1) & jnp.logical_not(is_away(p) & (z + 1 == nz - 1))

    def sends_left(p):
        return (z > 0) & jnp.logical_not(is_away(p) & (z - 1 == 0))

    def send_own(v):
        p = v // SPLIT
        when(sends_right(p), lambda: hop(z, z + 1, lambda s: go_right(v, z, s).start()))
        when(sends_left(p), lambda: hop(z, z - 1, lambda s: go_left(v, z, s).start()))

    def relay(v, first, last):
        p = v // SPLIT
        here = jnp.logical_not(is_away(p) & at_end)

        def one(d, carry):
            @pl.when((z - d >= 0) & here)
            def _():
                o = z - d
                hop(z - 1, z, lambda s: go_right(v, o, s).wait_recv())
                when(sends_right(p), lambda: hop(z, z + 1, lambda s: go_right(v, o, s).start()))
                hop(z - 1, z, lambda s: to_pair(v, o, s).start())

            @pl.when((z + d < nz) & here)
            def _():
                o = z + d
                hop(z + 1, z, lambda s: go_left(v, o, s).wait_recv())
                when(sends_left(p), lambda: hop(z, z - 1, lambda s: go_left(v, o, s).start()))
                hop(z + 1, z, lambda s: to_pair(v, o, s).start())

            return carry

        lax.fori_loop(first, last, one, 0)

    def drain(v):
        p = v // SPLIT

        def one(o, carry):
            when(
                (o <= z) & sends_right(p),
                lambda: hop(z, z + 1, lambda s: go_right(v, o, s).wait_send()),
            )
            when(
                (o >= z) & sends_left(p),
                lambda: hop(z, z - 1, lambda s: go_left(v, o, s).wait_send()),
            )

            @pl.when((o != z) & jnp.logical_not(is_away(p) & at_end))
            def _():
                hop(jnp.where(o < z, z - 1, z + 1), z, lambda s: to_pair(v, o, s).wait_send())

            return carry

        lax.fori_loop(0, nz, one, 0)

    def row_gather(buf, at, right, left, line, psend, precv):
        def block(o, core):
            return buf.at[2 * o + core, at, :]

        def to_right(o):
            return remote(block(o, c), block(o, c), right(o), line(o), {"tensor": t + 2})

        def to_left(o):
            return remote(block(o, c), block(o, c), left(o), line(o), {"tensor": t - 2})

        def across(o, core):
            return remote(
                block(o, core), block(o, core), psend(o), precv(o), {"tensor": 2 * x + 1 - c}
            )

        def begin():
            when(x < nx - 1, lambda: to_right(x).start())
            when(x > 0, lambda: to_left(x).start())
            across(x, c).start()

        def finish():
            for d in range(1, nx):
                @pl.when(x - d >= 0)
                def _(d=d):
                    to_right(x - d).wait_recv()
                    when(x < nx - 1, lambda: to_right(x - d).start())
                    across(x - d, c).start()

                @pl.when(x + d < nx)
                def _(d=d):
                    to_left(x + d).wait_recv()
                    when(x > 0, lambda: to_left(x + d).start())
                    across(x + d, c).start()

        def land():
            for o in range(nx):
                across(o, 1 - c).wait_recv()

        def settle():
            for o in range(nx):
                across(o, c).wait_send()
                when((o <= x) & (x < nx - 1), lambda o=o: to_right(o).wait_send())
                when((o >= x) & (x > 0), lambda o=o: to_left(o).wait_send())

        return begin, finish, land, settle

    def own_block(r):
        return row_gather(
            xbuf, pl.ds(pl.multiple_of(r * row_block, row_block), row_block),
            lambda o: x_right.at[r, o], lambda o: x_left.at[r, o], lambda o: x_line.at[r, o],
            lambda o: x_psend.at[r, o], lambda o: x_precv.at[r, o],
        )

    def span_rows(j):
        return pl.ds(pl.multiple_of(j * srows, srows), srows)

    def lend(j):
        at = span_rows(j)
        return remote(
            xbuf.at[t, at, :], sbuf.at[t, at, :], s_send.at[j], s_recv.at[j], {"cand": inner}
        )

    def borrowed(j):
        return row_gather(
            sbuf, span_rows(j), lambda o: sx_right.at[j, o], lambda o: sx_left.at[j, o],
            lambda o: sx_line.at[j, o], lambda o: sx_psend.at[j, o], lambda o: sx_precv.at[j, o],
        )

    def tile_rows(i):
        return pl.ds(pl.multiple_of(i * qrows, qrows), qrows)

    def give_back(g, i):
        at = tile_rows(i)
        return remote(
            sres.at[g, at, :], acts.at[first_away + g, at, :], r_send.at[g, i], r_recv.at[g, i],
            {"cand": outer},
        )

    def get_back(g, i):
        at = acts.at[first_away + g, tile_rows(i), :]
        return remote(at, at, r_send.at[g, i], r_recv.at[g, i], {"cand": inner})

    def each(first, last, body):
        def one(j, carry):
            body(j)
            return carry

        lax.fori_loop(first, last, one, 0)

    def others(body):
        each(1, nz, lambda d: body(lax.rem(z + d, nz)))

    def ask(src, buf, send, recv, o, lands):
        return remote(src, buf.at[lands], send.at[o], recv.at[lands], {"cand": o})

    def ask_all(o):
        ask(probes_ref, qall, q_send, q_recv, o, z).start()
        ask(pairs_ref, pall, p_send, p_recv, o, z).start()

    others(ask_all)
    for v in range(AHEAD):
        if v % SPLIT == 0:
            loads[v // SPLIT].wait()
        send_own(v)
    x_load.wait()
    for r in range(BLOCKS):
        own_block(r)[0]()
    for p in range(-(-AHEAD // SPLIT), nchunk):
        loads[p].wait()

    @pl.when(at_end)
    def _():
        def queue(v):
            send_own(v)
            j = v // per_lot - BEHIND
            when((lax.rem(v, per_lot) == per_lot - 1) & (j >= 0), lambda: lend(j).start())

        each(AHEAD, nv, queue)
        each(lots - BEHIND, lots, lambda j: lend(j).start())

    part[...] = jnp.zeros_like(part)

    lanes, fresh, _ = probes_ref.shape
    kv_here = pcache_ref.shape[2]
    tokens = pcache_ref.shape[1]
    pgroup = probes_ref.shape[2] // HD // kv_here
    prow = pgroup * fresh

    def match(o, l, b):
        same = kept_ref[o * lanes + l] == z * cands + b
        return jnp.where(same, 1.0, 0.0)

    def pick(o, q, kv, fresh_start):
        for b in range(cands):
            for l in range(lanes):
                m = match(o, l, b)
                if fresh_start and l == 0:
                    qsel[b] = q(l) * m
                    psel[b] = kv(l) * m
                else:
                    qsel[b] += q(l) * m
                    psel[b] += kv(l) * m

    def policy():
        pick(
            z, lambda l: probes_ref[l].astype(jnp.float32),
            lambda l: pairs_ref[l].astype(jnp.float32), True,
        )

        def take(o):
            ask(probes_ref, qall, q_send, q_recv, o, o).wait_recv()
            ask(pairs_ref, pall, p_send, p_recv, o, o).wait_recv()
            pick(
                o, lambda l: qall[o, l].astype(jnp.float32),
                lambda l: pall[o, l].astype(jnp.float32), False,
            )
            ask(probes_ref, qall, q_send, q_recv, o, z).wait_send()
            ask(pairs_ref, pall, p_send, p_recv, o, z).wait_send()

        others(take)
        for b in range(cands):
            for g in range(kv_here):
                for h in range(pgroup):
                    head = (g * pgroup + h) * HD
                    qrow[g * prow + h * fresh:g * prow + (h + 1) * fresh, :] = (
                        qsel[b, :, head:head + HD]
                    )
                krow[g * fresh:(g + 1) * fresh, :] = psel[b, :, g * CW:g * CW + HD]
                vrow[g * fresh:(g + 1) * fresh, :] = psel[b, :, g * CW + HD:(g + 1) * CW]
            p_loads[b].wait()
            old_k = pbuf[:, :, :HD].reshape(tokens * kv_here, HD)
            old_v = pbuf[:, :, HD:].reshape(tokens * kv_here, HD)
            q = qrow[...].astype(jnp.bfloat16)
            dims = (((1,), (1,)), ((), ()))
            s1 = lax.dot_general(q, old_k, dims, preferred_element_type=jnp.float32)
            s2 = lax.dot_general(
                q, krow[...].astype(jnp.bfloat16), dims, preferred_element_type=jnp.float32
            )
            r1 = lax.broadcasted_iota(jnp.int32, s1.shape, 0)
            c1 = lax.broadcasted_iota(jnp.int32, s1.shape, 1)
            r2 = lax.broadcasted_iota(jnp.int32, s2.shape, 0)
            c2 = lax.broadcasted_iota(jnp.int32, s2.shape, 1)
            live = extents_ref[z * cands + b]
            seen1 = (c1 % kv_here == r1 // prow) & (c1 < live * kv_here)
            seen2 = (c2 // fresh == r2 // prow) & (c2 % fresh <= r2 % fresh)
            s1 = jnp.where(seen1, s1, masked_value)
            s2 = jnp.where(seen2, s2, masked_value)
            top = jnp.maximum(
                jnp.max(s1, axis=1, keepdims=True), jnp.max(s2, axis=1, keepdims=True)
            )
            e1 = jnp.exp((s1 - top) * HD ** -0.5)
            e2 = jnp.exp((s2 - top) * HD ** -0.5)
            total = jnp.sum(e1, axis=1, keepdims=True) + jnp.sum(e2, axis=1, keepdims=True)
            out = jnp.dot(e1.astype(jnp.bfloat16), old_v, preferred_element_type=jnp.float32)
            out = out + jnp.dot(
                e2.astype(jnp.bfloat16), vrow[...].astype(jnp.bfloat16),
                preferred_element_type=jnp.float32,
            )
            if b + 1 < cands:
                p_loads[b + 1].start()
            out = out / total
            for o in range(nz):
                for l in range(lanes):
                    given_to = (out * match(o, l, b)).astype(jnp.bfloat16)
                    if b == 0:
                        placed[o, l] = given_to
                    else:
                        placed[o, l] += given_to

    def give(o):
        return remote(
            placed.at[o], given.at[z], give_send.at[o], give_recv.at[z], {"cand": o}
        )

    def get(o):
        return remote(
            placed.at[o], given.at[o], give_send.at[o], give_recv.at[o], {"cand": o}
        )

    def collect():
        mine[...] = placed[z].astype(jnp.float32)

        def add(o):
            get(o).wait_recv()
            mine[...] += given[o].astype(jnp.float32)
            give(o).wait_send()

        others(add)
        for l in range(lanes):
            for g in range(kv_here):
                for h in range(pgroup):
                    head = (g * pgroup + h) * HD
                    start = g * prow + h * fresh
                    mix_ref[l, :, head:head + HD] = (
                        mine[l, start:start + fresh, :].astype(mix_ref.dtype)
                    )

    policy()

    def multiply(buf, p, at):
        acc = jnp.dot(buf[0, at, :], wbuf[p, :dx, :], preferred_element_type=jnp.float32)
        for s in range(1, nt):
            acc = acc + jnp.dot(
                buf[s, at, :], wbuf[p, s * dx:(s + 1) * dx, :],
                preferred_element_type=jnp.float32,
            )
        return acc.astype(jnp.bfloat16)

    def project(n):
        p = lookup([u[0] for u in units["multiply"]], n)
        r = lookup([u[1] for u in units["multiply"]], n)

        @pl.when(jnp.logical_not(is_away(p) & at_end))
        def _():
            def take(d):
                o = jnp.where(d < z, d, d + 1)
                src = jnp.where(o < z, z - 1, z + 1)
                for q in range(SPLIT):
                    hop(src, z, lambda s: from_pair(p * SPLIT + q, o, s).wait_recv())

            when(r == 0, lambda: each(0, nz - 1, take))
            at = pl.ds(pl.multiple_of(r * row_block, row_block), row_block)
            acts[p, at, :] = multiply(xbuf, p, at)

    def lent_unit(n):
        g = lookup([u[0] for u in units["lent"]], n)
        i = lookup([u[1] for u in units["lent"]], n)
        return g, i

    def project_lent(n):
        g, i = lent_unit(n)

        @pl.when(g == 0)
        def _():
            first = (i * lots + TILES - 1) // TILES
            last = ((i + 1) * lots + TILES - 1) // TILES
            @pl.when(i == TILES - 1)
            def _():
                borrowed(lots - 2)[1]()
                borrowed(lots - 1)[1]()

            each(first, last, lambda j: borrowed(j)[2]())

        at = tile_rows(i)
        sres[g, at, :] = multiply(sbuf, first_away + g, at)

    def attend(p, i):
        g = group_of(p)
        j = jnp.where(is_away(p), qchunks - 1, lax.rem(p, qchunks) - 1)
        head0 = (g * qchunks + j) * 2
        base = pl.multiple_of(g * CW, CW)
        b = i // per_cand
        start = (i - b * per_cand) * qrows
        at = tile_rows(i)
        new_at = pl.ds(pl.multiple_of(b * span, span), span)
        q = jnp.concatenate([acts[p, at, :HD], acts[p, at, HD:]], axis=0)
        dims = (((1,), (1,)), ((), ()))
        scale = HD ** -0.5 * LOG2E

        def scores(keys):
            return lax.dot_general(q, keys, dims, preferred_element_type=jnp.float32)

        def weigh(e, values):
            both = jnp.concatenate([values, jnp.ones_like(values)], axis=1)
            return jnp.dot(e.astype(jnp.bfloat16), both, preferred_element_type=jnp.float32)

        s = scores(acts[g * qchunks, new_at, :HD])
        ri = lax.broadcasted_iota(jnp.int32, s.shape, 0)
        ci = lax.broadcasted_iota(jnp.int32, s.shape, 1)
        ri = jnp.where(ri >= qrows, ri - qrows, ri) + start
        s = jnp.where(ri >= ci, s, masked_value)
        top = jnp.max(s, axis=1, keepdims=True)
        o = weigh(jnp.exp2((s - top) * scale), acts[g * qchunks, new_at, HD:])
        for first in range(0, cbuf.shape[1], KEYS):
            keys = pl.ds(first, min(KEYS, cbuf.shape[1] - first))
            s = scores(cbuf[b, keys, pl.ds(base, HD)])
            higher = jnp.maximum(top, jnp.max(s, axis=1, keepdims=True))
            o = o * jnp.exp2((top - higher) * scale)
            top = higher
            o = o + weigh(
                jnp.exp2((s - top) * scale), cbuf[b, keys, pl.ds(pl.multiple_of(base + HD, HD), HD)]
            )
        o = o[:, :HD] / o[:, HD:]
        part[b, pl.ds(pl.multiple_of(start, qrows), qrows), :] += (
            o[:qrows] * grade_ref[pl.ds(head0, 1), :]
            + o[qrows:] * grade_ref[pl.ds(head0 + 1, 1), :]
        )

    def take_lot(j):
        lend(j).wait_recv()
        borrowed(j)[0]()
        when((j > 0) & (j < lots - 1), lambda: borrowed(j - 1)[1]())

    def compute(v, half):
        w = 2 * v + half
        when(beside & (w == 2 * nv - 1), lambda: take_lot(lots - 2))

        def between(kind):
            return lookup(ends[kind], w), lookup(ends[kind], w + 1)

        @pl.when(beside & (w > 0))
        def _():
            def send_back(n):
                g, i = lent_unit(n)
                give_back(g, i).start()

            each(lookup(ends["lent"], w - 1), lookup(ends["lent"], w), send_back)

        each(*between("multiply"), project)

        @pl.when(beside)
        def _():
            each(*between("lent"), project_lent)

        when(beside & (w == 2 * nv - 1), lambda: take_lot(lots - 1))
        a_lo, a_hi = between("attend")
        b_lo, b_hi = lookup(ends["back"], v), lookup(ends["back"], v + 1)
        ours = a_hi - a_lo
        theirs = jnp.where(at_end & (half == 0), b_hi - b_lo, 0)

        def unit(n):
            own = n < ours
            k = b_lo + n - ours
            g_back = lookup([u[0] for u in units["back"]], k)
            i_back = lookup([u[1] for u in units["back"]], k)
            p_own = lookup([u[0] for u in units["attend"]], a_lo + n)
            i_own = lookup([u[1] for u in units["attend"]], a_lo + n)
            p = jnp.where(own, p_own, first_away + g_back)
            i = jnp.where(own, i_own, i_back)
            when(jnp.logical_not(own), lambda: get_back(g_back, i_back).wait_recv())

            @pl.when(jnp.logical_not(own & is_away(p) & at_end))
            def _():
                attend(p, i)

        each(0, ours + theirs, unit)

    def step(v, carry):
        ongoing = v < nv

        each(
            jnp.where(v == 0, 0, v + LEAD), jnp.minimum(v + LEAD + 1, nv), lambda u: relay(u, 1, 2)
        )

        @pl.when((v + AHEAD < nv) & jnp.logical_not(at_end))
        def _():
            send_own(v + AHEAD)

        @pl.when(v == 1)
        def _():
            others(lambda o: give(o).start())

        when(v == nv + 1, collect)

        for r in range(BLOCKS):
            @pl.when(v == x_step[r])
            def _(r=r):
                own_block(r)[1]()
                own_block(r)[2]()

        when(v == x_step[0], c_load.wait)

        def rest(half, carry):
            compute(v, half)
            j = v // per_lot - BEHIND
            due = ongoing & (half == 0) & (lax.rem(v, per_lot) == per_lot - 1) & (j >= 0)
            when(beside & due, lambda: take_lot(j))

            @pl.when(ongoing & (half == 0))
            def _():
                relay(v, 2, min(3, nz))

            return carry

        lax.fori_loop(0, 2, rest, 0)
        when(ongoing, lambda: relay(v, 3, nz))

        when(v >= LAG, lambda: drain(v - LAG))
        return carry

    lax.fori_loop(0, nv + 2, step, 0)

    for b in range(cands):
        toks[t, b:b + 1, :] = jnp.sum(part[b].T, axis=0, keepdims=True)
    each(nv + 2 - LAG, nv, drain)
    for r in range(BLOCKS):
        own_block(r)[3]()

    def tell(o):
        return remote(toks.at[t], toks.at[t], t_send.at[o], t_recv.at[t], {"tensor": o})

    def hear(o):
        return remote(toks.at[o], toks.at[o], t_send.at[o], t_recv.at[o], {"tensor": o})

    each(1, nt, lambda d: tell(lax.rem(t + d, nt)).start())
    when(at_end, lambda: each(0, lots, lambda j: lend(j).wait_send()))

    @pl.when(beside)
    def _():
        each(0, lots, lambda j: borrowed(j)[3]())
        each(0, groups, lambda g: each(0, TILES, lambda i: give_back(g, i).wait_send()))

    def heard(d):
        o = lax.rem(t + d, nt)
        hear(o).wait_recv()
        tell(o).wait_send()

    each(1, nt, heard)
    total = toks[0]
    for o in range(1, nt):
        total = total + toks[o]
    reward_ref[...] = total


def local(
    nz, nt,
    response_latest_embeddings,
    critic_probe_projector,
    critic_pair_projector,
    critic_stored_pairs,
    critic_grading_vector,
    actor_stored_pairs,
    filled_extents,
    kept_responses,
    actor_latest_probes,
    actor_latest_pairs,
):
    cands, span, dx = response_latest_embeddings.shape
    rows = cands * span
    wq, wkv = critic_probe_projector, critic_pair_projector
    depth = wq.shape[0] * nz
    groups = wkv.shape[1] // CW
    per_group = wq.shape[1] // HD // groups
    nchunk = (wq.shape[1] + wkv.shape[1]) // CW
    nv = nchunk * SPLIT
    lots = 2 * nchunk
    nx = nt // 2
    lanes, fresh, pwidth = actor_latest_probes.shape
    kv_here = actor_stored_pairs.shape[2]
    prows = pwidth // HD * fresh
    bf16, f32 = jnp.bfloat16, jnp.float32
    vmem = pl.BlockSpec(memory_space=pltpu.VMEM)
    smem = pl.BlockSpec(memory_space=pltpu.SMEM)
    anywhere = pl.BlockSpec(memory_space=pl.ANY)
    dma = pltpu.SemaphoreType.DMA
    token_rewards, mixed = pl.pallas_call(
        functools.partial(reward_kernel, nz, nt, per_group),
        out_shape=(
            jax.ShapeDtypeStruct((cands, span), f32),
            jax.ShapeDtypeStruct(actor_latest_probes.shape, bf16),
        ),
        in_specs=[anywhere] * 5 + [vmem] * 3 + [smem] * 2,
        out_specs=(vmem, vmem),
        scratch_shapes=[
            pltpu.VMEM((nt, rows, dx), bf16),
            pltpu.VMEM((nt, rows, dx), bf16),
            pltpu.VMEM((nchunk, depth, CW), bf16),
            pltpu.VMEM(critic_stored_pairs.shape, bf16),
            pltpu.VMEM(actor_stored_pairs.shape[1:], bf16),
            pltpu.VMEM((nchunk, rows, CW), bf16),
            pltpu.VMEM((groups, rows, CW), bf16),
            pltpu.VMEM((cands, span, HD), f32),
            pltpu.VMEM((nt, cands, span), f32),
            pltpu.VMEM((nz,) + actor_latest_probes.shape, bf16),
            pltpu.VMEM((nz,) + actor_latest_pairs.shape, bf16),
            pltpu.VMEM((cands, fresh, pwidth), f32),
            pltpu.VMEM((cands, fresh, actor_latest_pairs.shape[2]), f32),
            pltpu.VMEM((prows, HD), f32),
            pltpu.VMEM((kv_here * fresh, HD), f32),
            pltpu.VMEM((kv_here * fresh, HD), f32),
            pltpu.VMEM((nz, lanes, prows, HD), bf16),
            pltpu.VMEM((nz, lanes, prows, HD), bf16),
            pltpu.VMEM((lanes, prows, HD), f32),
            dma((nchunk + 2 + cands,)),
            dma((nv, nz)), dma((nv, nz)), dma((nv, nz)), dma((nv, nz)), dma((nv, nz)),
            dma((BLOCKS, nx)), dma((BLOCKS, nx)), dma((BLOCKS, nx)), dma((BLOCKS, nx)), dma((BLOCKS, nx)),
            dma((lots,)), dma((lots,)),
            dma((lots, nx)), dma((lots, nx)), dma((lots, nx)), dma((lots, nx)), dma((lots, nx)),
            dma((groups, TILES)), dma((groups, TILES)),
            dma((nt,)), dma((nt,)),
            dma((nz,)), dma((nz,)), dma((nz,)), dma((nz,)), dma((nz,)), dma((nz,)),
        ],
        compiler_params=pltpu.CompilerParams(
            collective_id=0, has_side_effects=True, vmem_limit_bytes=67043328
        ),
    )(
        response_latest_embeddings.reshape(rows, dx), wq, wkv, critic_stored_pairs,
        actor_stored_pairs, critic_grading_vector.reshape(-1, HD), actor_latest_probes,
        actor_latest_pairs, kept_responses, filled_extents,
    )
    return token_rewards, mixed


def solution(mesh):
    placed = (
        P(("groups", "cand"), None, "tensor"),
        P("cand", "tensor"),
        P("cand", "tensor"),
        P(("groups", "cand"), None, "tensor"),
        P("tensor"),
        P(("groups", "cand"), None, "tensor", None),
        P("groups"),
        P("groups"),
        P(("groups", "cand"), None, "tensor"),
        P(("groups", "cand"), None, "tensor"),
    )
    return jax.shard_map(
        functools.partial(local, mesh.shape["cand"], mesh.shape["tensor"]),
        mesh=mesh,
        in_specs=placed,
        out_specs=(P(("groups", "cand"), None), P(("groups", "cand"), None, "tensor")),
        check_vma=False,
    )
```

```python
import functools

import jax
import jax.numpy as jnp
from jax import lax
from jax.experimental import pallas as pl
from jax.experimental.pallas import tpu as pltpu
from jax.sharding import PartitionSpec as P

HD = 128
CW = 2 * HD
SPLIT = 2
AHEAD = 2
LEAD = 1
BEHIND = 2
LAG = 2 * SPLIT
TILES = 4
BLOCKS = 3
ROOM = 4.0
KEYS = 512
MIDDLE = 0.594
COST = {"multiply": 1.3, "attend": 1.7, "lent": 1.0}
MESH = pl.DeviceIdType.MESH

masked_value = -1e30
LOG2E = 1.4426950408889634


def when(cond, body):
    pl.when(cond)(body)


def lookup(table, n):
    value = jnp.int32(table[0])
    for k in range(1, len(table)):
        if table[k] != table[k - 1]:
            value = jnp.where(n >= k, table[k], value)
    return value


def plan(nchunk, stride, cands):
    nv = nchunk * SPLIT
    groups = nchunk // stride
    early = stride - 1
    last = nchunk - 1
    first_away = groups * early
    x_step = [max(1, k * nv // 12) for k in (2, 4, 6)]
    lent_step = [k * nv // 12 for k in (6, 8, 11)] + [nv + 1]
    per_cand = TILES // cands
    todo_p = sorted(
        (max(2 * SPLIT * (p + 1) + 2, 2 * x_step[r]), p, r)
        for p in range(nchunk) for r in range(BLOCKS)
    )
    todo_p = [(min(w, 2 * nv + (p == last and r > 0)), p, r) for w, p, r in todo_p]
    todo_s = sorted(
        (max(min(2 * SPLIT * (first_away + g + 1) + 2, 2 * nv), 2 * lent_step[i]), i, g)
        for g in range(groups) for i in range(TILES)
    )
    todo_a = [
        (p, i) for p in range(nchunk) for i in range(TILES) if p >= first_away or p % early
    ]
    units = {"multiply": [], "attend": [], "lent": []}
    ends = {k: [0] for k in units}
    done = {}
    lent_at = {}

    def blocks(first, last):
        return range(first * BLOCKS // TILES, -(-last * BLOCKS // TILES))

    for w in range(2 * (nv + 2)):
        left = ROOM if w < 2 * nv - 1 else 1e9
        while todo_p and todo_p[0][0] <= w and left > 0:
            _, p, r = todo_p.pop(0)
            units["multiply"].append((p, r))
            done[p, r] = w
            left -= COST["multiply"]
        while todo_s and todo_s[0][0] <= w and left > 0:
            _, i, g = todo_s[0]
            if (first_away + g, 0) not in done:
                break
            todo_s.pop(0)
            units["lent"].append((g, i))
            lent_at[g, i] = w // 2
            left -= COST["lent"]
        if w >= 2 * nv - 1:
            left = 99 if w in (2 * nv - 1, 2 * nv + 3) else 0
            left = left * COST["attend"] - 0.1
        while todo_a and left > 0:
            ready = None
            for p, i in todo_a:
                b = i // per_cand
                need = [(p, r) for r in blocks(i, i + 1)]
                kv = p // early * early if p < first_away else (p - first_away) * early
                need += [(kv, r) for r in blocks(b * per_cand, (b + 1) * per_cand)]
                if all(n in done for n in need):
                    ready = (p, i)
                    break
            if ready is None:
                break
            todo_a.remove(ready)
            units["attend"].append(ready)
            left -= COST["attend"]
        for k in units:
            ends[k].append(len(units[k]))
    assert not (todo_p or todo_s or todo_a)
    back = sorted(
        (lent_at[u] + 2 if lent_at[u] + 2 <= nv else nv + 1, lent_at[u], u[1], u[0]) for u in units["lent"]
    )
    units["back"] = [(g, i) for _, _, i, g in back]
    ends["back"] = [sum(b[0] < v for b in back) for v in range(nv + 3)]
    return units, ends, x_step


def reward_kernel(
    nz, nt, per_group,
    x_ref, wq_ref, wkv_ref, cache_ref, pcache_ref,
    grade_ref, probes_ref, pairs_ref, kept_ref, extents_ref,
    reward_ref, mix_ref,
    xbuf, sbuf, wbuf, cbuf, pbuf, acts, sres, part, toks,
    qall, pall, qsel, psel, qrow, krow, vrow, placed, given, mine,
    load_sem, right_sem, left_sem, line_sem, pair_send, pair_recv,
    x_right, x_left, x_line, x_psend, x_precv,
    s_send, s_recv, sx_right, sx_left, sx_line, sx_psend, sx_precv,
    r_send, r_recv, t_send, t_recv,
    q_send, q_recv, p_send, p_recv, give_send, give_recv,
):
    nchunk, depth, _ = wbuf.shape
    nv = nchunk * SPLIT
    dz = depth // nz
    sub = dz // SPLIT
    nx = nt // 2
    cands, span, _ = part.shape
    rows = cands * span
    dx = depth // nt
    qchunks = per_group * HD // CW
    groups = nchunk // (1 + qchunks)
    qrows = rows // TILES
    per_cand = TILES // cands
    lots = 2 * nchunk
    per_lot = SPLIT // 2
    srows = rows // lots
    stride = 1 + qchunks
    row_block = rows // BLOCKS
    first_away = groups * qchunks
    units, ends, x_step = plan(nchunk, stride, cands)

    def whole16(n):
        return max(sub // 2, int(round(n / 16)) * 16)

    share_first = whole16(sub * 2 / 3)
    share_mid = whole16(sub * MIDDLE)
    share_last = sub // 2

    y = lax.axis_index("groups")
    z = lax.axis_index("cand")
    t = lax.axis_index("tensor")
    x = t // 2
    c = t - 2 * x
    at_end = (z == 0) | (z == nz - 1)
    beside = (z == 1) | (z == nz - 2)
    inner = jnp.where(z == 0, 1, nz - 2)
    outer = jnp.where(z == 1, 0, nz - 1)

    def is_away(p):
        return p >= first_away

    def group_of(p):
        return jnp.where(is_away(p), p - first_away, p // qchunks)

    def columns(p):
        if p >= first_away:
            g, j = p - first_away, qchunks - 1
        else:
            g, j = p // qchunks, p % qchunks - 1
        if j < 0:
            return wkv_ref.at[:, pl.ds(g * CW, CW)]
        return wq_ref.at[:, pl.ds((g * qchunks + j) * CW, CW)]

    own_rows = pl.ds(pl.multiple_of(z * dz, dz), dz)
    loads = [
        pltpu.make_async_copy(columns(p), wbuf.at[p, own_rows, :], load_sem.at[p])
        for p in range(nchunk)
    ]
    x_load = pltpu.make_async_copy(x_ref, xbuf.at[t], load_sem.at[nchunk])
    c_load = pltpu.make_async_copy(cache_ref, cbuf, load_sem.at[nchunk + 1])
    p_loads = [
        pltpu.make_async_copy(pcache_ref.at[b], pbuf, load_sem.at[nchunk + 2 + b])
        for b in range(cands)
    ]
    loads[0].start()
    x_load.start()
    for p in range(1, nchunk):
        loads[p].start()
    p_loads[0].start()
    c_load.start()

    barrier = pltpu.get_barrier_semaphore()

    def greet(device):
        pl.semaphore_signal(barrier, inc=1, device_id=device, device_id_type=MESH)

    greet({"groups": 1 - y})

    def greet_cand(d, carry):
        greet({"cand": lax.rem(z + d, nz)})
        return carry

    def greet_tensor(d, carry):
        greet({"tensor": lax.rem(t + d, nt)})
        return carry

    lax.fori_loop(1, nz, greet_cand, 0)
    lax.fori_loop(1, nt, greet_tensor, 0)
    pl.semaphore_wait(barrier, nz + nt - 1)

    def remote(src, dst, send, recv, device):
        return pltpu.make_async_remote_copy(
            src_ref=src, dst_ref=dst, send_sem=send, recv_sem=recv,
            device_id=device, device_id_type=MESH,
        )

    def hop(src, dst, body):
        first = (src == 0) | (src == nz - 1)
        last = (dst == 0) | (dst == nz - 1)
        when(first, lambda: body(share_first))
        when(last, lambda: body(share_last))
        when(jnp.logical_not(first | last), lambda: body(share_mid))

    def piece(v, o, start, size):
        p = v // SPLIT
        base = o * dz + (v - p * SPLIT) * sub + start
        return wbuf.at[p, pl.ds(pl.multiple_of(base, 16), size), :]

    def go_right(v, o, s):
        ref = piece(v, o, y * (sub - s), s)
        return remote(ref, ref, right_sem.at[v, o], line_sem.at[v, o], {"cand": z + 1})

    def go_left(v, o, s):
        ref = piece(v, o, y * (sub - s), s)
        return remote(ref, ref, left_sem.at[v, o], line_sem.at[v, o], {"cand": z - 1})

    def to_pair(v, o, s):
        ref = piece(v, o, y * s, sub - s)
        return remote(ref, ref, pair_send.at[v, o], pair_recv.at[v, o], {"groups": 1 - y})

    def from_pair(v, o, s):
        ref = piece(v, o, (1 - y) * s, sub - s)
        return remote(ref, ref, pair_send.at[v, o], pair_recv.at[v, o], {"groups": 1 - y})

    def sends_right(p):
        return (z < nz - 1) & jnp.logical_not(is_away(p) & (z + 1 == nz - 1))

    def sends_left(p):
        return (z > 0) & jnp.logical_not(is_away(p) & (z - 1 == 0))

    def send_own(v):
        p = v // SPLIT
        when(sends_right(p), lambda: hop(z, z + 1, lambda s: go_right(v, z, s).start()))
        when(sends_left(p), lambda: hop(z, z - 1, lambda s: go_left(v, z, s).start()))

    def relay(v, first, last):
        p = v // SPLIT
        here = jnp.logical_not(is_away(p) & at_end)

        def one(d, carry):
            @pl.when((z - d >= 0) & here)
            def _():
                o = z - d
                hop(z - 1, z, lambda s: go_right(v, o, s).wait_recv())
                when(sends_right(p), lambda: hop(z, z + 1, lambda s: go_right(v, o, s).start()))
                hop(z - 1, z, lambda s: to_pair(v, o, s).start())

            @pl.when((z + d < nz) & here)
            def _():
                o = z + d
                hop(z + 1, z, lambda s: go_left(v, o, s).wait_recv())
                when(sends_left(p), lambda: hop(z, z - 1, lambda s: go_left(v, o, s).start()))
                hop(z + 1, z, lambda s: to_pair(v, o, s).start())

            return carry

        lax.fori_loop(first, last, one, 0)

    def drain(v):
        p = v // SPLIT

        def one(o, carry):
            when(
                (o <= z) & sends_right(p),
                lambda: hop(z, z + 1, lambda s: go_right(v, o, s).wait_send()),
            )
            when(
                (o >= z) & sends_left(p),
                lambda: hop(z, z - 1, lambda s: go_left(v, o, s).wait_send()),
            )

            @pl.when((o != z) & jnp.logical_not(is_away(p) & at_end))
            def _():
                hop(jnp.where(o < z, z - 1, z + 1), z, lambda s: to_pair(v, o, s).wait_send())

            return carry

        lax.fori_loop(0, nz, one, 0)

    def row_gather(buf, at, right, left, line, psend, precv):
        def block(o, core):
            return buf.at[2 * o + core, at, :]

        def to_right(o):
            return remote(block(o, c), block(o, c), right(o), line(o), {"tensor": t + 2})

        def to_left(o):
            return remote(block(o, c), block(o, c), left(o), line(o), {"tensor": t - 2})

        def across(o, core):
            return remote(
                block(o, core), block(o, core), psend(o), precv(o), {"tensor": 2 * x + 1 - c}
            )

        def begin():
            when(x < nx - 1, lambda: to_right(x).start())
            when(x > 0, lambda: to_left(x).start())
            across(x, c).start()

        def finish():
            for d in range(1, nx):
                @pl.when(x - d >= 0)
                def _(d=d):
                    to_right(x - d).wait_recv()
                    when(x < nx - 1, lambda: to_right(x - d).start())
                    across(x - d, c).start()

                @pl.when(x + d < nx)
                def _(d=d):
                    to_left(x + d).wait_recv()
                    when(x > 0, lambda: to_left(x + d).start())
                    across(x + d, c).start()

        def land():
            for o in range(nx):
                across(o, 1 - c).wait_recv()

        def settle():
            for o in range(nx):
                across(o, c).wait_send()
                when((o <= x) & (x < nx - 1), lambda o=o: to_right(o).wait_send())
                when((o >= x) & (x > 0), lambda o=o: to_left(o).wait_send())

        return begin, finish, land, settle

    def own_block(r):
        return row_gather(
            xbuf, pl.ds(pl.multiple_of(r * row_block, row_block), row_block),
            lambda o: x_right.at[r, o], lambda o: x_left.at[r, o], lambda o: x_line.at[r, o],
            lambda o: x_psend.at[r, o], lambda o: x_precv.at[r, o],
        )

    def span_rows(j):
        return pl.ds(pl.multiple_of(j * srows, srows), srows)

    def lend(j):
        at = span_rows(j)
        return remote(
            xbuf.at[t, at, :], sbuf.at[t, at, :], s_send.at[j], s_recv.at[j], {"cand": inner}
        )

    def borrowed(j):
        return row_gather(
            sbuf, span_rows(j), lambda o: sx_right.at[j, o], lambda o: sx_left.at[j, o],
            lambda o: sx_line.at[j, o], lambda o: sx_psend.at[j, o], lambda o: sx_precv.at[j, o],
        )

    def tile_rows(i):
        return pl.ds(pl.multiple_of(i * qrows, qrows), qrows)

    def give_back(g, i):
        at = tile_rows(i)
        return remote(
            sres.at[g, at, :], acts.at[first_away + g, at, :], r_send.at[g, i], r_recv.at[g, i],
            {"cand": outer},
        )

    def get_back(g, i):
        at = acts.at[first_away + g, tile_rows(i), :]
        return remote(at, at, r_send.at[g, i], r_recv.at[g, i], {"cand": inner})

    def each(first, last, body):
        def one(j, carry):
            body(j)
            return carry

        lax.fori_loop(first, last, one, 0)

    def others(body):
        each(1, nz, lambda d: body(lax.rem(z + d, nz)))

    def ask(src, buf, send, recv, o, lands):
        return remote(src, buf.at[lands], send.at[o], recv.at[lands], {"cand": o})

    def ask_all(o):
        ask(probes_ref, qall, q_send, q_recv, o, z).start()
        ask(pairs_ref, pall, p_send, p_recv, o, z).start()

    others(ask_all)
    for v in range(AHEAD):
        if v % SPLIT == 0:
            loads[v // SPLIT].wait()
        send_own(v)
    x_load.wait()
    for r in range(BLOCKS):
        own_block(r)[0]()
    for p in range(-(-AHEAD // SPLIT), nchunk):
        loads[p].wait()

    @pl.when(at_end)
    def _():
        def queue(v):
            send_own(v)
            j = v // per_lot - BEHIND
            when((lax.rem(v, per_lot) == per_lot - 1) & (j >= 0), lambda: lend(j).start())

        each(AHEAD, nv, queue)
        each(lots - BEHIND, lots, lambda j: lend(j).start())

    part[...] = jnp.zeros_like(part)

    lanes, fresh, _ = probes_ref.shape
    kv_here = pcache_ref.shape[2]
    tokens = pcache_ref.shape[1]
    pgroup = probes_ref.shape[2] // HD // kv_here
    prow = pgroup * fresh

    def match(o, l, b):
        same = kept_ref[o * lanes + l] == z * cands + b
        return jnp.where(same, 1.0, 0.0)

    def pick(o, q, kv, fresh_start):
        for b in range(cands):
            for l in range(lanes):
                m = match(o, l, b)
                if fresh_start and l == 0:
                    qsel[b] = q(l) * m
                    psel[b] = kv(l) * m
                else:
                    qsel[b] += q(l) * m
                    psel[b] += kv(l) * m

    def policy():
        pick(
            z, lambda l: probes_ref[l].astype(jnp.float32),
            lambda l: pairs_ref[l].astype(jnp.float32), True,
        )

        def take(o):
            ask(probes_ref, qall, q_send, q_recv, o, o).wait_recv()
            ask(pairs_ref, pall, p_send, p_recv, o, o).wait_recv()
            pick(
                o, lambda l: qall[o, l].astype(jnp.float32),
                lambda l: pall[o, l].astype(jnp.float32), False,
            )
            ask(probes_ref, qall, q_send, q_recv, o, z).wait_send()
            ask(pairs_ref, pall, p_send, p_recv, o, z).wait_send()

        others(take)
        for b in range(cands):
            for g in range(kv_here):
                for h in range(pgroup):
                    head = (g * pgroup + h) * HD
                    qrow[g * prow + h * fresh:g * prow + (h + 1) * fresh, :] = (
                        qsel[b, :, head:head + HD]
                    )
                krow[g * fresh:(g + 1) * fresh, :] = psel[b, :, g * CW:g * CW + HD]
                vrow[g * fresh:(g + 1) * fresh, :] = psel[b, :, g * CW + HD:(g + 1) * CW]
            p_loads[b].wait()
            old_k = pbuf[:, :, :HD].reshape(tokens * kv_here, HD)
            old_v = pbuf[:, :, HD:].reshape(tokens * kv_here, HD)
            q = qrow[...].astype(jnp.bfloat16)
            dims = (((1,), (1,)), ((), ()))
            s1 = lax.dot_general(q, old_k, dims, preferred_element_type=jnp.float32)
            s2 = lax.dot_general(
                q, krow[...].astype(jnp.bfloat16), dims, preferred_element_type=jnp.float32
            )
            r1 = lax.broadcasted_iota(jnp.int32, s1.shape, 0)
            c1 = lax.broadcasted_iota(jnp.int32, s1.shape, 1)
            r2 = lax.broadcasted_iota(jnp.int32, s2.shape, 0)
            c2 = lax.broadcasted_iota(jnp.int32, s2.shape, 1)
            live = extents_ref[z * cands + b]
            seen1 = (c1 % kv_here == r1 // prow) & (c1 < live * kv_here)
            seen2 = (c2 // fresh == r2 // prow) & (c2 % fresh <= r2 % fresh)
            s1 = jnp.where(seen1, s1, masked_value)
            s2 = jnp.where(seen2, s2, masked_value)
            top = jnp.maximum(
                jnp.max(s1, axis=1, keepdims=True), jnp.max(s2, axis=1, keepdims=True)
            )
            e1 = jnp.exp((s1 - top) * HD ** -0.5)
            e2 = jnp.exp((s2 - top) * HD ** -0.5)
            total = jnp.sum(e1, axis=1, keepdims=True) + jnp.sum(e2, axis=1, keepdims=True)
            out = jnp.dot(e1.astype(jnp.bfloat16), old_v, preferred_element_type=jnp.float32)
            out = out + jnp.dot(
                e2.astype(jnp.bfloat16), vrow[...].astype(jnp.bfloat16),
                preferred_element_type=jnp.float32,
            )
            if b + 1 < cands:
                p_loads[b + 1].start()
            out = out / total
            for o in range(nz):
                for l in range(lanes):
                    given_to = (out * match(o, l, b)).astype(jnp.bfloat16)
                    if b == 0:
                        placed[o, l] = given_to
                    else:
                        placed[o, l] += given_to

    def give(o):
        return remote(
            placed.at[o], given.at[z], give_send.at[o], give_recv.at[z], {"cand": o}
        )

    def get(o):
        return remote(
            placed.at[o], given.at[o], give_send.at[o], give_recv.at[o], {"cand": o}
        )

    def collect():
        mine[...] = placed[z].astype(jnp.float32)

        def add(o):
            get(o).wait_recv()
            mine[...] += given[o].astype(jnp.float32)
            give(o).wait_send()

        others(add)
        for l in range(lanes):
            for g in range(kv_here):
                for h in range(pgroup):
                    head = (g * pgroup + h) * HD
                    start = g * prow + h * fresh
                    mix_ref[l, :, head:head + HD] = (
                        mine[l, start:start + fresh, :].astype(mix_ref.dtype)
                    )

    policy()

    def multiply(buf, p, at):
        acc = jnp.dot(buf[0, at, :], wbuf[p, :dx, :], preferred_element_type=jnp.float32)
        for s in range(1, nt):
            acc = acc + jnp.dot(
                buf[s, at, :], wbuf[p, s * dx:(s + 1) * dx, :],
                preferred_element_type=jnp.float32,
            )
        return acc.astype(jnp.bfloat16)

    def project(n):
        p = lookup([u[0] for u in units["multiply"]], n)
        r = lookup([u[1] for u in units["multiply"]], n)

        @pl.when(jnp.logical_not(is_away(p) & at_end))
        def _():
            def take(d):
                o = jnp.where(d < z, d, d + 1)
                src = jnp.where(o < z, z - 1, z + 1)
                for q in range(SPLIT):
                    hop(src, z, lambda s: from_pair(p * SPLIT + q, o, s).wait_recv())

            when(r == 0, lambda: each(0, nz - 1, take))
            at = pl.ds(pl.multiple_of(r * row_block, row_block), row_block)
            acts[p, at, :] = multiply(xbuf, p, at)

    def lent_unit(n):
        g = lookup([u[0] for u in units["lent"]], n)
        i = lookup([u[1] for u in units["lent"]], n)
        return g, i

    def project_lent(n):
        g, i = lent_unit(n)

        @pl.when(g == 0)
        def _():
            first = (i * lots + TILES - 1) // TILES
            last = ((i + 1) * lots + TILES - 1) // TILES
            @pl.when(i == TILES - 1)
            def _():
                borrowed(lots - 2)[1]()
                borrowed(lots - 1)[1]()

            each(first, last, lambda j: borrowed(j)[2]())

        at = tile_rows(i)
        sres[g, at, :] = multiply(sbuf, first_away + g, at)

    def attend(p, i):
        g = group_of(p)
        j = jnp.where(is_away(p), qchunks - 1, lax.rem(p, qchunks) - 1)
        head0 = (g * qchunks + j) * 2
        base = pl.multiple_of(g * CW, CW)
        b = i // per_cand
        start = (i - b * per_cand) * qrows
        at = tile_rows(i)
        new_at = pl.ds(pl.multiple_of(b * span, span), span)
        q = jnp.concatenate([acts[p, at, :HD], acts[p, at, HD:]], axis=0)
        dims = (((1,), (1,)), ((), ()))
        scale = HD ** -0.5 * LOG2E

        def scores(keys):
            return lax.dot_general(q, keys, dims, preferred_element_type=jnp.float32)

        def weigh(e, values):
            both = jnp.concatenate([values, jnp.ones_like(values)], axis=1)
            return jnp.dot(e.astype(jnp.bfloat16), both, preferred_element_type=jnp.float32)

        s = scores(acts[g * qchunks, new_at, :HD])
        ri = lax.broadcasted_iota(jnp.int32, s.shape, 0)
        ci = lax.broadcasted_iota(jnp.int32, s.shape, 1)
        ri = jnp.where(ri >= qrows, ri - qrows, ri) + start
        s = jnp.where(ri >= ci, s, masked_value)
        top = jnp.max(s, axis=1, keepdims=True)
        o = weigh(jnp.exp2((s - top) * scale), acts[g * qchunks, new_at, HD:])
        for first in range(0, cbuf.shape[1], KEYS):
            keys = pl.ds(first, min(KEYS, cbuf.shape[1] - first))
            s = scores(cbuf[b, keys, pl.ds(base, HD)])
            higher = jnp.maximum(top, jnp.max(s, axis=1, keepdims=True))
            o = o * jnp.exp2((top - higher) * scale)
            top = higher
            o = o + weigh(
                jnp.exp2((s - top) * scale), cbuf[b, keys, pl.ds(pl.multiple_of(base + HD, HD), HD)]
            )
        o = o[:, :HD] / o[:, HD:]
        part[b, pl.ds(pl.multiple_of(start, qrows), qrows), :] += (
            o[:qrows] * grade_ref[pl.ds(head0, 1), :]
            + o[qrows:] * grade_ref[pl.ds(head0 + 1, 1), :]
        )

    def take_lot(j):
        lend(j).wait_recv()
        borrowed(j)[0]()
        when((j > 0) & (j < lots - 1), lambda: borrowed(j - 1)[1]())

    def compute(v, half):
        w = 2 * v + half
        when(beside & (w == 2 * nv), lambda: take_lot(lots - 1))

        def between(kind):
            return lookup(ends[kind], w), lookup(ends[kind], w + 1)

        @pl.when(beside & (w > 0))
        def _():
            def send_back(n):
                g, i = lent_unit(n)
                give_back(g, i).start()

            each(lookup(ends["lent"], w - 1), lookup(ends["lent"], w), send_back)

        each(*between("multiply"), project)

        @pl.when(beside)
        def _():
            each(*between("lent"), project_lent)

        when(beside & (w == 2 * nv - 1), lambda: take_lot(lots - 2))
        a_lo, a_hi = between("attend")
        b_lo, b_hi = lookup(ends["back"], v), lookup(ends["back"], v + 1)
        ours = a_hi - a_lo
        theirs = jnp.where(at_end & (half == 0), b_hi - b_lo, 0)

        def unit(n):
            own = n < ours
            k = b_lo + n - ours
            g_back = lookup([u[0] for u in units["back"]], k)
            i_back = lookup([u[1] for u in units["back"]], k)
            p_own = lookup([u[0] for u in units["attend"]], a_lo + n)
            i_own = lookup([u[1] for u in units["attend"]], a_lo + n)
            p = jnp.where(own, p_own, first_away + g_back)
            i = jnp.where(own, i_own, i_back)
            when(jnp.logical_not(own), lambda: get_back(g_back, i_back).wait_recv())

            @pl.when(jnp.logical_not(own & is_away(p) & at_end))
            def _():
                attend(p, i)

        each(0, ours + theirs, unit)

    def step(v, carry):
        ongoing = v < nv

        each(
            jnp.where(v == 0, 0, v + LEAD), jnp.minimum(v + LEAD + 1, nv), lambda u: relay(u, 1, 2)
        )

        @pl.when((v + AHEAD < nv) & jnp.logical_not(at_end))
        def _():
            send_own(v + AHEAD)

        @pl.when(v == 1)
        def _():
            others(lambda o: give(o).start())

        when(v == nv + 1, collect)

        for r in range(BLOCKS):
            @pl.when(v == x_step[r])
            def _(r=r):
                own_block(r)[1]()
                own_block(r)[2]()

        when(v == x_step[0], c_load.wait)

        def rest(half, carry):
            compute(v, half)
            j = v // per_lot - BEHIND
            due = ongoing & (half == 0) & (lax.rem(v, per_lot) == per_lot - 1) & (j >= 0)
            when(beside & due, lambda: take_lot(j))

            @pl.when(ongoing & (half == 0))
            def _():
                relay(v, 2, min(3, nz))

            return carry

        lax.fori_loop(0, 2, rest, 0)
        when(ongoing, lambda: relay(v, 3, nz))

        when(v >= LAG, lambda: drain(v - LAG))
        return carry

    lax.fori_loop(0, nv + 2, step, 0)

    for b in range(cands):
        toks[t, b:b + 1, :] = jnp.sum(part[b].T, axis=0, keepdims=True)
    each(nv + 2 - LAG, nv, drain)
    for r in range(BLOCKS):
        own_block(r)[3]()

    def tell(o):
        return remote(toks.at[t], toks.at[t], t_send.at[o], t_recv.at[t], {"tensor": o})

    def hear(o):
        return remote(toks.at[o], toks.at[o], t_send.at[o], t_recv.at[o], {"tensor": o})

    each(1, nt, lambda d: tell(lax.rem(t + d, nt)).start())
    when(at_end, lambda: each(0, lots, lambda j: lend(j).wait_send()))

    @pl.when(beside)
    def _():
        each(0, lots, lambda j: borrowed(j)[3]())
        each(0, groups, lambda g: each(0, TILES, lambda i: give_back(g, i).wait_send()))

    def heard(d):
        o = lax.rem(t + d, nt)
        hear(o).wait_recv()
        tell(o).wait_send()

    each(1, nt, heard)
    total = toks[0]
    for o in range(1, nt):
        total = total + toks[o]
    reward_ref[...] = total


def local(
    nz, nt,
    response_latest_embeddings,
    critic_probe_projector,
    critic_pair_projector,
    critic_stored_pairs,
    critic_grading_vector,
    actor_stored_pairs,
    filled_extents,
    kept_responses,
    actor_latest_probes,
    actor_latest_pairs,
):
    cands, span, dx = response_latest_embeddings.shape
    rows = cands * span
    wq, wkv = critic_probe_projector, critic_pair_projector
    depth = wq.shape[0] * nz
    groups = wkv.shape[1] // CW
    per_group = wq.shape[1] // HD // groups
    nchunk = (wq.shape[1] + wkv.shape[1]) // CW
    nv = nchunk * SPLIT
    lots = 2 * nchunk
    nx = nt // 2
    lanes, fresh, pwidth = actor_latest_probes.shape
    kv_here = actor_stored_pairs.shape[2]
    prows = pwidth // HD * fresh
    bf16, f32 = jnp.bfloat16, jnp.float32
    vmem = pl.BlockSpec(memory_space=pltpu.VMEM)
    smem = pl.BlockSpec(memory_space=pltpu.SMEM)
    anywhere = pl.BlockSpec(memory_space=pl.ANY)
    dma = pltpu.SemaphoreType.DMA
    token_rewards, mixed = pl.pallas_call(
        functools.partial(reward_kernel, nz, nt, per_group),
        out_shape=(
            jax.ShapeDtypeStruct((cands, span), f32),
            jax.ShapeDtypeStruct(actor_latest_probes.shape, bf16),
        ),
        in_specs=[anywhere] * 5 + [vmem] * 3 + [smem] * 2,
        out_specs=(vmem, vmem),
        scratch_shapes=[
            pltpu.VMEM((nt, rows, dx), bf16),
            pltpu.VMEM((nt, rows, dx), bf16),
            pltpu.VMEM((nchunk, depth, CW), bf16),
            pltpu.VMEM(critic_stored_pairs.shape, bf16),
            pltpu.VMEM(actor_stored_pairs.shape[1:], bf16),
            pltpu.VMEM((nchunk, rows, CW), bf16),
            pltpu.VMEM((groups, rows, CW), bf16),
            pltpu.VMEM((cands, span, HD), f32),
            pltpu.VMEM((nt, cands, span), f32),
            pltpu.VMEM((nz,) + actor_latest_probes.shape, bf16),
            pltpu.VMEM((nz,) + actor_latest_pairs.shape, bf16),
            pltpu.VMEM((cands, fresh, pwidth), f32),
            pltpu.VMEM((cands, fresh, actor_latest_pairs.shape[2]), f32),
            pltpu.VMEM((prows, HD), f32),
            pltpu.VMEM((kv_here * fresh, HD), f32),
            pltpu.VMEM((kv_here * fresh, HD), f32),
            pltpu.VMEM((nz, lanes, prows, HD), bf16),
            pltpu.VMEM((nz, lanes, prows, HD), bf16),
            pltpu.VMEM((lanes, prows, HD), f32),
            dma((nchunk + 2 + cands,)),
            dma((nv, nz)), dma((nv, nz)), dma((nv, nz)), dma((nv, nz)), dma((nv, nz)),
            dma((BLOCKS, nx)), dma((BLOCKS, nx)), dma((BLOCKS, nx)), dma((BLOCKS, nx)), dma((BLOCKS, nx)),
            dma((lots,)), dma((lots,)),
            dma((lots, nx)), dma((lots, nx)), dma((lots, nx)), dma((lots, nx)), dma((lots, nx)),
            dma((groups, TILES)), dma((groups, TILES)),
            dma((nt,)), dma((nt,)),
            dma((nz,)), dma((nz,)), dma((nz,)), dma((nz,)), dma((nz,)), dma((nz,)),
        ],
        compiler_params=pltpu.CompilerParams(
            collective_id=0, has_side_effects=True, vmem_limit_bytes=67043328
        ),
    )(
        response_latest_embeddings.reshape(rows, dx), wq, wkv, critic_stored_pairs,
        actor_stored_pairs, critic_grading_vector.reshape(-1, HD), actor_latest_probes,
        actor_latest_pairs, kept_responses, filled_extents,
    )
    return token_rewards, mixed


def solution(mesh):
    placed = (
        P(("groups", "cand"), None, "tensor"),
        P("cand", "tensor"),
        P("cand", "tensor"),
        P(("groups", "cand"), None, "tensor"),
        P("tensor"),
        P(("groups", "cand"), None, "tensor", None),
        P("groups"),
        P("groups"),
        P(("groups", "cand"), None, "tensor"),
        P(("groups", "cand"), None, "tensor"),
    )
    return jax.shard_map(
        functools.partial(local, mesh.shape["cand"], mesh.shape["tensor"]),
        mesh=mesh,
        in_specs=placed,
        out_specs=(P(("groups", "cand"), None), P(("groups", "cand"), None, "tensor")),
        check_vma=False,
    )
```

```python
import functools

import jax
import jax.numpy as jnp
from jax import lax
from jax.experimental import pallas as pl
from jax.experimental.pallas import tpu as pltpu
from jax.sharding import PartitionSpec as P

HD = 128
CW = 2 * HD
SPLIT = 2
AHEAD = 2
LEAD = 1
BEHIND = 2
LAG = 2 * SPLIT
WINDOW = LEAD + LAG + 1
TILES = 4
BLOCKS = 3
ROOM = 4.0
KEYS = 256
MIDDLE = 0.594
COST = {"multiply": 1.3, "attend": 1.7, "lent": 1.0}
MESH = pl.DeviceIdType.MESH

masked_value = -1e30
LOG2E = 1.4426950408889634


def when(cond, body):
    pl.when(cond)(body)


def lookup(table, n):
    value = jnp.int32(table[0])
    for k in range(1, len(table)):
        if table[k] != table[k - 1]:
            value = jnp.where(n >= k, table[k], value)
    return value


def plan(nchunk, stride, cands):
    nv = nchunk * SPLIT
    groups = nchunk // stride
    early = stride - 1
    last = nchunk - 1
    first_away = groups * early
    x_step = [max(1, k * nv // 12) for k in (2, 4, 6)]
    lent_step = [k * nv // 12 for k in (6, 8, 11)] + [nv + 1]
    per_cand = TILES // cands
    todo_p = sorted(
        (max(2 * SPLIT * (p + 1) + 2, 2 * x_step[r]), p, r)
        for p in range(nchunk) for r in range(BLOCKS)
    )
    todo_p = [(min(w, 2 * nv + (p == last and r > 0)), p, r) for w, p, r in todo_p]
    todo_s = sorted(
        (max(min(2 * SPLIT * (first_away + g + 1) + 2, 2 * nv), 2 * lent_step[i]), i, g)
        for g in range(groups) for i in range(TILES)
    )
    todo_a = [
        (p, i) for p in range(nchunk) for i in range(TILES) if p >= first_away or p % early
    ]
    units = {"multiply": [], "attend": [], "lent": []}
    ends = {k: [0] for k in units}
    done = {}
    lent_at = {}

    def blocks(first, last):
        return range(first * BLOCKS // TILES, -(-last * BLOCKS // TILES))

    for w in range(2 * (nv + 2)):
        left = ROOM if w < 2 * nv - 1 else 1e9
        while todo_p and todo_p[0][0] <= w and left > 0:
            _, p, r = todo_p.pop(0)
            units["multiply"].append((p, r))
            done[p, r] = w
            left -= COST["multiply"]
        while todo_s and todo_s[0][0] <= w and left > 0:
            _, i, g = todo_s[0]
            if (first_away + g, 0) not in done:
                break
            todo_s.pop(0)
            units["lent"].append((g, i))
            lent_at[g, i] = w // 2
            left -= COST["lent"]
        if w >= 2 * nv - 1:
            left = 99 if w in (2 * nv - 1, 2 * nv + 3) else 0
            left = left * COST["attend"] - 0.1
        while todo_a and left > 0:
            ready = None
            for p, i in todo_a:
                b = i // per_cand
                need = [(p, r) for r in blocks(i, i + 1)]
                kv = p // early * early if p < first_away else (p - first_away) * early
                need += [(kv, r) for r in blocks(b * per_cand, (b + 1) * per_cand)]
                if all(n in done for n in need):
                    ready = (p, i)
                    break
            if ready is None:
                break
            todo_a.remove(ready)
            units["attend"].append(ready)
            left -= COST["attend"]
        for k in units:
            ends[k].append(len(units[k]))
    assert not (todo_p or todo_s or todo_a)
    back = sorted(
        (lent_at[u] + 2 if lent_at[u] + 2 <= nv else nv + 1, lent_at[u], u[1], u[0]) for u in units["lent"]
    )
    units["back"] = [(g, i) for _, _, i, g in back]
    ends["back"] = [sum(b[0] < v for b in back) for v in range(nv + 3)]
    return units, ends, x_step


def reward_kernel(
    nz, nt, per_group,
    x_ref, wq_ref, wkv_ref, cache_ref, pcache_ref,
    grade_ref, probes_ref, pairs_ref, kept_ref, extents_ref,
    reward_ref, mix_ref,
    xbuf, sbuf, wbuf, cbuf, pbuf, acts, sres, part, toks,
    qall, pall, qsel, psel, qrow, krow, vrow, placed, given, mine,
    load_sem, hop_sem, line_sem, pair_send, pair_recv,
    x_hop, x_line, x_psend, x_precv,
    s_recv, sx_hop, sx_line, sx_psend, sx_precv,
    r_send, r_recv, t_send, t_recv,
    q_send, q_recv, p_send, p_recv, give_send, give_recv,
):
    nchunk, depth, _ = wbuf.shape
    nv = nchunk * SPLIT
    dz = depth // nz
    sub = dz // SPLIT
    nx = nt // 2
    cands, span, _ = part.shape
    rows = cands * span
    dx = depth // nt
    qchunks = per_group * HD // CW
    groups = nchunk // (1 + qchunks)
    qrows = rows // TILES
    per_cand = TILES // cands
    lots = 2 * nchunk
    per_lot = SPLIT // 2
    srows = rows // lots
    stride = 1 + qchunks
    row_block = rows // BLOCKS
    first_away = groups * qchunks
    units, ends, x_step = plan(nchunk, stride, cands)

    def whole16(n):
        return max(sub // 2, int(round(n / 16)) * 16)

    share_first = whole16(sub * 2 / 3)
    share_mid = whole16(sub * MIDDLE)
    share_last = sub // 2

    y = lax.axis_index("groups")
    z = lax.axis_index("cand")
    t = lax.axis_index("tensor")
    x = t // 2
    c = t - 2 * x
    at_end = (z == 0) | (z == nz - 1)
    beside = (z == 1) | (z == nz - 2)
    inner = jnp.where(z == 0, 1, nz - 2)
    outer = jnp.where(z == 1, 0, nz - 1)

    def is_away(p):
        return p >= first_away

    def group_of(p):
        return jnp.where(is_away(p), p - first_away, p // qchunks)

    def columns(p):
        if p >= first_away:
            g, j = p - first_away, qchunks - 1
        else:
            g, j = p // qchunks, p % qchunks - 1
        if j < 0:
            return wkv_ref.at[:, pl.ds(g * CW, CW)]
        return wq_ref.at[:, pl.ds((g * qchunks + j) * CW, CW)]

    own_rows = pl.ds(pl.multiple_of(z * dz, dz), dz)
    loads = [
        pltpu.make_async_copy(columns(p), wbuf.at[p, own_rows, :], load_sem.at[p])
        for p in range(nchunk)
    ]
    x_load = pltpu.make_async_copy(x_ref, xbuf.at[t], load_sem.at[nchunk])
    c_load = pltpu.make_async_copy(cache_ref, cbuf, load_sem.at[nchunk + 1])
    p_loads = [
        pltpu.make_async_copy(pcache_ref.at[b], pbuf, load_sem.at[nchunk + 2 + b])
        for b in range(cands)
    ]
    loads[0].start()
    x_load.start()
    for p in range(1, nchunk):
        loads[p].start()
    p_loads[0].start()
    c_load.start()

    barrier = pltpu.get_barrier_semaphore()

    def greet(device):
        pl.semaphore_signal(barrier, inc=1, device_id=device, device_id_type=MESH)

    greet({"groups": 1 - y})

    def greet_cand(d, carry):
        greet({"cand": lax.rem(z + d, nz)})
        return carry

    def greet_tensor(d, carry):
        greet({"tensor": lax.rem(t + d, nt)})
        return carry

    lax.fori_loop(1, nz, greet_cand, 0)
    lax.fori_loop(1, nt, greet_tensor, 0)
    pl.semaphore_wait(barrier, nz + nt - 1)

    def remote(src, dst, send, recv, device):
        return pltpu.make_async_remote_copy(
            src_ref=src, dst_ref=dst, send_sem=send, recv_sem=recv,
            device_id=device, device_id_type=MESH,
        )

    def hop(src, dst, body):
        first = (src == 0) | (src == nz - 1)
        last = (dst == 0) | (dst == nz - 1)
        when(first, lambda: body(share_first))
        when(last, lambda: body(share_last))
        when(jnp.logical_not(first | last), lambda: body(share_mid))

    def piece(v, o, start, size):
        p = v // SPLIT
        base = o * dz + (v - p * SPLIT) * sub + start
        return wbuf.at[p, pl.ds(pl.multiple_of(base, 16), size), :]

    def go_right(v, o, s):
        ref = piece(v, o, y * (sub - s), s)
        return remote(ref, ref, hop_sem.at[v, o], line_sem.at[v, o], {"cand": z + 1})

    def go_left(v, o, s):
        ref = piece(v, o, y * (sub - s), s)
        return remote(ref, ref, hop_sem.at[v, o + 1], line_sem.at[v, o], {"cand": z - 1})

    def to_pair(v, o, s):
        ref = piece(v, o, y * s, sub - s)
        return remote(ref, ref, pair_send.at[lax.rem(v, WINDOW), o], pair_recv.at[v, o], {"groups": 1 - y})

    def from_pair(v, o, s):
        ref = piece(v, o, (1 - y) * s, sub - s)
        return remote(ref, ref, pair_send.at[lax.rem(v, WINDOW), o], pair_recv.at[v, o], {"groups": 1 - y})

    def sends_right(p):
        return (z < nz - 1) & jnp.logical_not(is_away(p) & (z + 1 == nz - 1))

    def sends_left(p):
        return (z > 0) & jnp.logical_not(is_away(p) & (z - 1 == 0))

    def send_own(v):
        p = v // SPLIT
        when(sends_right(p), lambda: hop(z, z + 1, lambda s: go_right(v, z, s).start()))
        when(sends_left(p), lambda: hop(z, z - 1, lambda s: go_left(v, z, s).start()))

    def relay(v, first, last):
        p = v // SPLIT
        here = jnp.logical_not(is_away(p) & at_end)

        def one(d, carry):
            @pl.when((z - d >= 0) & here)
            def _():
                o = z - d
                hop(z - 1, z, lambda s: go_right(v, o, s).wait_recv())
                when(sends_right(p), lambda: hop(z, z + 1, lambda s: go_right(v, o, s).start()))
                hop(z - 1, z, lambda s: to_pair(v, o, s).start())

            @pl.when((z + d < nz) & here)
            def _():
                o = z + d
                hop(z + 1, z, lambda s: go_left(v, o, s).wait_recv())
                when(sends_left(p), lambda: hop(z, z - 1, lambda s: go_left(v, o, s).start()))
                hop(z + 1, z, lambda s: to_pair(v, o, s).start())

            return carry

        lax.fori_loop(first, last, one, 0)

    def drain(v):
        p = v // SPLIT

        def one(o, carry):
            when(
                (o <= z) & sends_right(p),
                lambda: hop(z, z + 1, lambda s: go_right(v, o, s).wait_send()),
            )
            when(
                (o >= z) & sends_left(p),
                lambda: hop(z, z - 1, lambda s: go_left(v, o, s).wait_send()),
            )

            @pl.when((o != z) & jnp.logical_not(is_away(p) & at_end))
            def _():
                hop(jnp.where(o < z, z - 1, z + 1), z, lambda s: to_pair(v, o, s).wait_send())

            return carry

        lax.fori_loop(0, nz, one, 0)

    def row_gather(buf, at, right, left, line, psend, precv):
        def block(o, core):
            return buf.at[2 * o + core, at, :]

        def to_right(o):
            return remote(block(o, c), block(o, c), right(o), line(o), {"tensor": t + 2})

        def to_left(o):
            return remote(block(o, c), block(o, c), left(o), line(o), {"tensor": t - 2})

        def across(o, core):
            return remote(
                block(o, core), block(o, core), psend(o), precv(o), {"tensor": 2 * x + 1 - c}
            )

        def begin():
            when(x < nx - 1, lambda: to_right(x).start())
            when(x > 0, lambda: to_left(x).start())
            across(x, c).start()

        def finish():
            for d in range(1, nx):
                @pl.when(x - d >= 0)
                def _(d=d):
                    to_right(x - d).wait_recv()
                    when(x < nx - 1, lambda: to_right(x - d).start())
                    across(x - d, c).start()

                @pl.when(x + d < nx)
                def _(d=d):
                    to_left(x + d).wait_recv()
                    when(x > 0, lambda: to_left(x + d).start())
                    across(x + d, c).start()

        def land():
            for o in range(nx):
                across(o, 1 - c).wait_recv()

        def settle():
            for o in range(nx):
                across(o, c).wait_send()
                when((o <= x) & (x < nx - 1), lambda o=o: to_right(o).wait_send())
                when((o >= x) & (x > 0), lambda o=o: to_left(o).wait_send())

        return begin, finish, land, settle

    def own_block(r):
        return row_gather(
            xbuf, pl.ds(pl.multiple_of(r * row_block, row_block), row_block),
            lambda o: x_hop.at[r, o], lambda o: x_hop.at[r, o + 1], lambda o: x_line.at[r, o],
            lambda o: x_psend.at[r, o], lambda o: x_precv.at[r, o],
        )

    def span_rows(j):
        return pl.ds(pl.multiple_of(j * srows, srows), srows)

    def lend(j):
        at = span_rows(j)
        return remote(
            xbuf.at[t, at, :], sbuf.at[t, at, :], sx_psend.at[j, 0], s_recv.at[j], {"cand": inner}
        )

    def borrowed(j):
        return row_gather(
            sbuf, span_rows(j), lambda o: sx_hop.at[j, o], lambda o: sx_hop.at[j, o + 1],
            lambda o: sx_line.at[j, o], lambda o: sx_psend.at[j, o], lambda o: sx_precv.at[j, o],
        )

    def tile_rows(i):
        return pl.ds(pl.multiple_of(i * qrows, qrows), qrows)

    def give_back(g, i):
        at = tile_rows(i)
        return remote(
            sres.at[g, at, :], acts.at[first_away + g, at, :], r_send.at[g, i], r_recv.at[g, i],
            {"cand": outer},
        )

    def get_back(g, i):
        at = acts.at[first_away + g, tile_rows(i), :]
        return remote(at, at, r_send.at[g, i], r_recv.at[g, i], {"cand": inner})

    def each(first, last, body):
        def one(j, carry):
            body(j)
            return carry

        lax.fori_loop(first, last, one, 0)

    def others(body):
        each(1, nz, lambda d: body(lax.rem(z + d, nz)))

    def ask(src, buf, send, recv, o, lands):
        return remote(src, buf.at[lands], send.at[o], recv.at[lands], {"cand": o})

    def ask_all(o):
        ask(probes_ref, qall, q_send, q_recv, o, z).start()
        ask(pairs_ref, pall, p_send, p_recv, o, z).start()

    others(ask_all)
    for v in range(AHEAD):
        if v % SPLIT == 0:
            loads[v // SPLIT].wait()
        send_own(v)
    x_load.wait()
    for r in range(BLOCKS):
        own_block(r)[0]()
    for p in range(-(-AHEAD // SPLIT), nchunk):
        loads[p].wait()

    @pl.when(at_end)
    def _():
        def queue(v):
            send_own(v)
            j = v // per_lot - BEHIND
            when((lax.rem(v, per_lot) == per_lot - 1) & (j >= 0), lambda: lend(j).start())

        each(AHEAD, nv, queue)
        each(lots - BEHIND, lots, lambda j: lend(j).start())

    part[...] = jnp.zeros_like(part)

    lanes, fresh, _ = probes_ref.shape
    kv_here = pcache_ref.shape[2]
    tokens = pcache_ref.shape[1]
    pgroup = probes_ref.shape[2] // HD // kv_here
    prow = pgroup * fresh

    def match(o, l, b):
        same = kept_ref[o * lanes + l] == z * cands + b
        return jnp.where(same, 1.0, 0.0)

    def pick(o, q, kv, fresh_start):
        for b in range(cands):
            for l in range(lanes):
                m = match(o, l, b)
                if fresh_start and l == 0:
                    qsel[b] = q(l) * m
                    psel[b] = kv(l) * m
                else:
                    qsel[b] += q(l) * m
                    psel[b] += kv(l) * m

    def policy():
        pick(
            z, lambda l: probes_ref[l].astype(jnp.float32),
            lambda l: pairs_ref[l].astype(jnp.float32), True,
        )

        def take(o):
            ask(probes_ref, qall, q_send, q_recv, o, o).wait_recv()
            ask(pairs_ref, pall, p_send, p_recv, o, o).wait_recv()
            pick(
                o, lambda l: qall[o, l].astype(jnp.float32),
                lambda l: pall[o, l].astype(jnp.float32), False,
            )
            ask(probes_ref, qall, q_send, q_recv, o, z).wait_send()
            ask(pairs_ref, pall, p_send, p_recv, o, z).wait_send()

        others(take)
        for b in range(cands):
            for g in range(kv_here):
                for h in range(pgroup):
                    head = (g * pgroup + h) * HD
                    qrow[g * prow + h * fresh:g * prow + (h + 1) * fresh, :] = (
                        qsel[b, :, head:head + HD]
                    )
                krow[g * fresh:(g + 1) * fresh, :] = psel[b, :, g * CW:g * CW + HD]
                vrow[g * fresh:(g + 1) * fresh, :] = psel[b, :, g * CW + HD:(g + 1) * CW]
            p_loads[b].wait()
            old_k = pbuf[:, :, :HD].reshape(tokens * kv_here, HD)
            old_v = pbuf[:, :, HD:].reshape(tokens * kv_here, HD)
            q = qrow[...].astype(jnp.bfloat16)
            dims = (((1,), (1,)), ((), ()))
            s1 = lax.dot_general(q, old_k, dims, preferred_element_type=jnp.float32)
            s2 = lax.dot_general(
                q, krow[...].astype(jnp.bfloat16), dims, preferred_element_type=jnp.float32
            )
            r1 = lax.broadcasted_iota(jnp.int32, s1.shape, 0)
            c1 = lax.broadcasted_iota(jnp.int32, s1.shape, 1)
            r2 = lax.broadcasted_iota(jnp.int32, s2.shape, 0)
            c2 = lax.broadcasted_iota(jnp.int32, s2.shape, 1)
            live = extents_ref[z * cands + b]
            seen1 = (c1 % kv_here == r1 // prow) & (c1 < live * kv_here)
            seen2 = (c2 // fresh == r2 // prow) & (c2 % fresh <= r2 % fresh)
            s1 = jnp.where(seen1, s1, masked_value)
            s2 = jnp.where(seen2, s2, masked_value)
            top = jnp.maximum(
                jnp.max(s1, axis=1, keepdims=True), jnp.max(s2, axis=1, keepdims=True)
            )
            e1 = jnp.exp((s1 - top) * HD ** -0.5)
            e2 = jnp.exp((s2 - top) * HD ** -0.5)
            total = jnp.sum(e1, axis=1, keepdims=True) + jnp.sum(e2, axis=1, keepdims=True)
            out = jnp.dot(e1.astype(jnp.bfloat16), old_v, preferred_element_type=jnp.float32)
            out = out + jnp.dot(
                e2.astype(jnp.bfloat16), vrow[...].astype(jnp.bfloat16),
                preferred_element_type=jnp.float32,
            )
            if b + 1 < cands:
                p_loads[b + 1].start()
            out = out / total
            for o in range(nz):
                for l in range(lanes):
                    given_to = (out * match(o, l, b)).astype(jnp.bfloat16)
                    if b == 0:
                        placed[o, l] = given_to
                    else:
                        placed[o, l] += given_to

    def give(o):
        return remote(
            placed.at[o], given.at[z], give_send.at[o], give_recv.at[z], {"cand": o}
        )

    def get(o):
        return remote(
            placed.at[o], given.at[o], give_send.at[o], give_recv.at[o], {"cand": o}
        )

    def collect():
        mine[...] = placed[z].astype(jnp.float32)

        def add(o):
            get(o).wait_recv()
            mine[...] += given[o].astype(jnp.float32)
            give(o).wait_send()

        others(add)
        for l in range(lanes):
            for g in range(kv_here):
                for h in range(pgroup):
                    head = (g * pgroup + h) * HD
                    start = g * prow + h * fresh
                    mix_ref[l, :, head:head + HD] = (
                        mine[l, start:start + fresh, :].astype(mix_ref.dtype)
                    )

    policy()

    def multiply(buf, p, at):
        acc = jnp.dot(buf[0, at, :], wbuf[p, :dx, :], preferred_element_type=jnp.float32)
        for s in range(1, nt):
            acc = acc + jnp.dot(
                buf[s, at, :], wbuf[p, s * dx:(s + 1) * dx, :],
                preferred_element_type=jnp.float32,
            )
        return acc.astype(jnp.bfloat16)

    def project(n):
        p = lookup([u[0] for u in units["multiply"]], n)
        r = lookup([u[1] for u in units["multiply"]], n)

        @pl.when(jnp.logical_not(is_away(p) & at_end))
        def _():
            def take(d):
                o = jnp.where(d < z, d, d + 1)
                src = jnp.where(o < z, z - 1, z + 1)
                for q in range(SPLIT):
                    hop(src, z, lambda s: from_pair(p * SPLIT + q, o, s).wait_recv())

            when(r == 0, lambda: each(0, nz - 1, take))
            at = pl.ds(pl.multiple_of(r * row_block, row_block), row_block)
            acts[p, at, :] = multiply(xbuf, p, at)

    def lent_unit(n):
        g = lookup([u[0] for u in units["lent"]], n)
        i = lookup([u[1] for u in units["lent"]], n)
        return g, i

    def project_lent(n):
        g, i = lent_unit(n)

        @pl.when(g == 0)
        def _():
            first = (i * lots + TILES - 1) // TILES
            last = ((i + 1) * lots + TILES - 1) // TILES
            @pl.when(i == TILES - 1)
            def _():
                borrowed(lots - 2)[1]()
                borrowed(lots - 1)[1]()

            each(first, last, lambda j: borrowed(j)[2]())

        at = tile_rows(i)
        sres[g, at, :] = multiply(sbuf, first_away + g, at)

    def attend(p, i):
        g = group_of(p)
        j = jnp.where(is_away(p), qchunks - 1, lax.rem(p, qchunks) - 1)
        head0 = (g * qchunks + j) * 2
        base = pl.multiple_of(g * CW, CW)
        b = i // per_cand
        start = (i - b * per_cand) * qrows
        at = tile_rows(i)
        new_at = pl.ds(pl.multiple_of(b * span, span), span)
        q = jnp.concatenate([acts[p, at, :HD], acts[p, at, HD:]], axis=0)
        dims = (((1,), (1,)), ((), ()))
        scale = HD ** -0.5 * LOG2E

        def scores(keys):
            return lax.dot_general(q, keys, dims, preferred_element_type=jnp.float32)

        def weigh(e, values):
            both = jnp.concatenate([values, jnp.ones_like(values)], axis=1)
            return jnp.dot(e.astype(jnp.bfloat16), both, preferred_element_type=jnp.float32)

        s = scores(acts[g * qchunks, new_at, :HD])
        ri = lax.broadcasted_iota(jnp.int32, s.shape, 0)
        ci = lax.broadcasted_iota(jnp.int32, s.shape, 1)
        ri = jnp.where(ri >= qrows, ri - qrows, ri) + start
        s = jnp.where(ri >= ci, s, masked_value)
        top = jnp.max(s, axis=1, keepdims=True)
        o = weigh(jnp.exp2((s - top) * scale), acts[g * qchunks, new_at, HD:])
        for first in range(0, cbuf.shape[1], KEYS):
            keys = pl.ds(first, min(KEYS, cbuf.shape[1] - first))
            s = scores(cbuf[b, keys, pl.ds(base, HD)])
            higher = jnp.maximum(top, jnp.max(s, axis=1, keepdims=True))
            o = o * jnp.exp2((top - higher) * scale)
            top = higher
            o = o + weigh(
                jnp.exp2((s - top) * scale), cbuf[b, keys, pl.ds(pl.multiple_of(base + HD, HD), HD)]
            )
        o = o[:, :HD] / o[:, HD:]
        part[b, pl.ds(pl.multiple_of(start, qrows), qrows), :] += (
            o[:qrows] * grade_ref[pl.ds(head0, 1), :]
            + o[qrows:] * grade_ref[pl.ds(head0 + 1, 1), :]
        )

    def take_lot(j):
        lend(j).wait_recv()
        borrowed(j)[0]()
        when((j > 0) & (j < lots - 1), lambda: borrowed(j - 1)[1]())

    def compute(v, half):
        w = 2 * v + half
        when(beside & (w == 2 * nv), lambda: take_lot(lots - 1))

        def between(kind):
            return lookup(ends[kind], w), lookup(ends[kind], w + 1)

        @pl.when(beside & (w > 0))
        def _():
            def send_back(n):
                g, i = lent_unit(n)
                give_back(g, i).start()

            each(lookup(ends["lent"], w - 1), lookup(ends["lent"], w), send_back)

        each(*between("multiply"), project)

        @pl.when(beside)
        def _():
            each(*between("lent"), project_lent)

        when(beside & (w == 2 * nv - 1), lambda: take_lot(lots - 2))
        a_lo, a_hi = between("attend")
        b_lo, b_hi = lookup(ends["back"], v), lookup(ends["back"], v + 1)
        ours = a_hi - a_lo
        theirs = jnp.where(at_end & (half == 0), b_hi - b_lo, 0)

        def unit(n):
            own = n < ours
            k = b_lo + n - ours
            g_back = lookup([u[0] for u in units["back"]], k)
            i_back = lookup([u[1] for u in units["back"]], k)
            p_own = lookup([u[0] for u in units["attend"]], a_lo + n)
            i_own = lookup([u[1] for u in units["attend"]], a_lo + n)
            p = jnp.where(own, p_own, first_away + g_back)
            i = jnp.where(own, i_own, i_back)
            when(jnp.logical_not(own), lambda: get_back(g_back, i_back).wait_recv())

            @pl.when(jnp.logical_not(own & is_away(p) & at_end))
            def _():
                attend(p, i)

        each(0, ours + theirs, unit)

    def step(v, carry):
        ongoing = v < nv

        each(
            jnp.where(v == 0, 0, v + LEAD), jnp.minimum(v + LEAD + 1, nv), lambda u: relay(u, 1, 2)
        )

        @pl.when((v + AHEAD < nv) & jnp.logical_not(at_end))
        def _():
            send_own(v + AHEAD)

        @pl.when(v == 1)
        def _():
            others(lambda o: give(o).start())

        when(v == nv + 1, collect)

        for r in range(BLOCKS):
            @pl.when(v == x_step[r])
            def _(r=r):
                own_block(r)[1]()
                own_block(r)[2]()

        when(v == x_step[0], c_load.wait)

        def rest(half, carry):
            compute(v, half)
            j = v // per_lot - BEHIND
            due = ongoing & (half == 0) & (lax.rem(v, per_lot) == per_lot - 1) & (j >= 0)
            when(beside & due, lambda: take_lot(j))

            @pl.when(ongoing & (half == 0))
            def _():
                relay(v, 2, min(3, nz))

            return carry

        lax.fori_loop(0, 2, rest, 0)
        when(ongoing, lambda: relay(v, 3, nz))

        when(v >= LAG, lambda: drain(v - LAG))
        return carry

    lax.fori_loop(0, nv + 2, step, 0)

    for b in range(cands):
        toks[t, b:b + 1, :] = jnp.sum(part[b].T, axis=0, keepdims=True)
    each(nv + 2 - LAG, nv, drain)
    for r in range(BLOCKS):
        own_block(r)[3]()

    def tell(o):
        return remote(toks.at[t], toks.at[t], t_send.at[o], t_recv.at[t], {"tensor": o})

    def hear(o):
        return remote(toks.at[o], toks.at[o], t_send.at[o], t_recv.at[o], {"tensor": o})

    each(1, nt, lambda d: tell(lax.rem(t + d, nt)).start())
    when(at_end, lambda: each(0, lots, lambda j: lend(j).wait_send()))

    @pl.when(beside)
    def _():
        each(0, lots, lambda j: borrowed(j)[3]())
        each(0, groups, lambda g: each(0, TILES, lambda i: give_back(g, i).wait_send()))

    def heard(d):
        o = lax.rem(t + d, nt)
        hear(o).wait_recv()
        tell(o).wait_send()

    each(1, nt, heard)
    total = toks[0]
    for o in range(1, nt):
        total = total + toks[o]
    reward_ref[...] = total


def local(
    nz, nt,
    response_latest_embeddings,
    critic_probe_projector,
    critic_pair_projector,
    critic_stored_pairs,
    critic_grading_vector,
    actor_stored_pairs,
    filled_extents,
    kept_responses,
    actor_latest_probes,
    actor_latest_pairs,
):
    cands, span, dx = response_latest_embeddings.shape
    rows = cands * span
    wq, wkv = critic_probe_projector, critic_pair_projector
    depth = wq.shape[0] * nz
    groups = wkv.shape[1] // CW
    per_group = wq.shape[1] // HD // groups
    nchunk = (wq.shape[1] + wkv.shape[1]) // CW
    nv = nchunk * SPLIT
    lots = 2 * nchunk
    nx = nt // 2
    lanes, fresh, pwidth = actor_latest_probes.shape
    kv_here = actor_stored_pairs.shape[2]
    prows = pwidth // HD * fresh
    bf16, f32 = jnp.bfloat16, jnp.float32
    vmem = pl.BlockSpec(memory_space=pltpu.VMEM)
    smem = pl.BlockSpec(memory_space=pltpu.SMEM)
    anywhere = pl.BlockSpec(memory_space=pl.ANY)
    dma = pltpu.SemaphoreType.DMA
    token_rewards, mixed = pl.pallas_call(
        functools.partial(reward_kernel, nz, nt, per_group),
        out_shape=(
            jax.ShapeDtypeStruct((cands, span), f32),
            jax.ShapeDtypeStruct(actor_latest_probes.shape, bf16),
        ),
        in_specs=[anywhere] * 5 + [vmem] * 3 + [smem] * 2,
        out_specs=(vmem, vmem),
        scratch_shapes=[
            pltpu.VMEM((nt, rows, dx), bf16),
            pltpu.VMEM((nt, rows, dx), bf16),
            pltpu.VMEM((nchunk, depth, CW), bf16),
            pltpu.VMEM(critic_stored_pairs.shape, bf16),
            pltpu.VMEM(actor_stored_pairs.shape[1:], bf16),
            pltpu.VMEM((nchunk, rows, CW), bf16),
            pltpu.VMEM((groups, rows, CW), bf16),
            pltpu.VMEM((cands, span, HD), f32),
            pltpu.VMEM((nt, cands, span), f32),
            pltpu.VMEM((nz,) + actor_latest_probes.shape, bf16),
            pltpu.VMEM((nz,) + actor_latest_pairs.shape, bf16),
            pltpu.VMEM((cands, fresh, pwidth), f32),
            pltpu.VMEM((cands, fresh, actor_latest_pairs.shape[2]), f32),
            pltpu.VMEM((prows, HD), f32),
            pltpu.VMEM((kv_here * fresh, HD), f32),
            pltpu.VMEM((kv_here * fresh, HD), f32),
            pltpu.VMEM((nz, lanes, prows, HD), bf16),
            pltpu.VMEM((nz, lanes, prows, HD), bf16),
            pltpu.VMEM((lanes, prows, HD), f32),
            dma((nchunk + 2 + cands,)),
            dma((nv, nz + 1)), dma((nv, nz)), dma((WINDOW, nz)), dma((nv, nz)),
            dma((BLOCKS, nx + 1)), dma((BLOCKS, nx)), dma((BLOCKS, nx)), dma((BLOCKS, nx)),
            dma((lots,)),
            dma((lots, nx + 1)), dma((lots, nx)), dma((lots, nx)), dma((lots, nx)),
            dma((groups, TILES)), dma((groups, TILES)),
            dma((nt,)), dma((nt,)),
            dma((nz,)), dma((nz,)), dma((nz,)), dma((nz,)), dma((nz,)), dma((nz,)),
        ],
        compiler_params=pltpu.CompilerParams(
            collective_id=0, has_side_effects=True, vmem_limit_bytes=67043328
        ),
    )(
        response_latest_embeddings.reshape(rows, dx), wq, wkv, critic_stored_pairs,
        actor_stored_pairs, critic_grading_vector.reshape(-1, HD), actor_latest_probes,
        actor_latest_pairs, kept_responses, filled_extents,
    )
    return token_rewards, mixed


def solution(mesh):
    placed = (
        P(("groups", "cand"), None, "tensor"),
        P("cand", "tensor"),
        P("cand", "tensor"),
        P(("groups", "cand"), None, "tensor"),
        P("tensor"),
        P(("groups", "cand"), None, "tensor", None),
        P("groups"),
        P("groups"),
        P(("groups", "cand"), None, "tensor"),
        P(("groups", "cand"), None, "tensor"),
    )
    return jax.shard_map(
        functools.partial(local, mesh.shape["cand"], mesh.shape["tensor"]),
        mesh=mesh,
        in_specs=placed,
        out_specs=(P(("groups", "cand"), None), P(("groups", "cand"), None, "tensor")),
        check_vma=False,
    )
```
